256 devices in a mesh: energy: 32 (over y, x, core), orb: 8 (over z).
Axes of the slice: x: 4, y: 4, z: 8, core: 2. Of those that a mesh axis runs over, the one named last changes fastest.
Arguments:
- green: float32 [32, 2, 2048, 2048], P('energy', None, 'orb'), may hold values from -0.75 to 0.75
- sigma: float32 [32, 16, 2, 128, 128], P('energy', 'orb'), may hold values from -0.375 to 0.375
- neighbours: int32 [256, 16], P('orb'), may hold values from 0 to 255, as said below
- phonon_shift: int32 [6], replicated, may hold values from 1 to 16
- phonon_weight: float32 [2, 6], replicated, may hold values from 0.1 to 0.6
- dham: float32 [4096, 3, 8, 8], P('orb'), may hold values from -2 to 2
Outputs:
- scattering: float32 [32, 4096, 128], P('energy', 'orb')
The draws below stay inside these ranges and needn't reach their ends.
Inputs may be any that keep to these rules, and one draw needn't show every extreme that they name: neighbours[a, k] is an atom other than a within 8 atoms of a; every atom has a neighbour exactly 8 atoms away.
All inputs are finite; a program needn't handle non-finite values.
Results may differ from the reference program's by a relative error of at most 0.0003.
Values sent between devices are 32-bit elements; how exact they have to be, the bound alone decides.
A program may use at most 128 MiB of HBM per device.

```python
import math
import jax
import jax.numpy as jnp
from jax import lax

N = 2048
W = 8
BS = 128
K = 16
REACH = 8
Q = 6
NE = 32
NA = 256
PAIRS = 4096
SHIFT_MAX = 16


def draw_neighbours(key, part):
    atom_ids = jnp.arange(NA, dtype=jnp.int32)
    partner = atom_ids + 1 - 2 * (atom_ids % 2)
    distant = jnp.where(atom_ids + REACH < NA, atom_ids + REACH, atom_ids - REACH)
    key_step, key_side = jax.random.split(jax.random.fold_in(key, 11))
    stride = jax.random.randint(key_step, (NA, K - 2), 1, REACH + 1, dtype=jnp.int32)
    direction = 2 * jax.random.randint(key_side, (NA, K - 2), 0, 2, dtype=jnp.int32) - 1
    ahead = atom_ids[:, None] + direction * stride
    inside = (ahead >= 0) & (ahead < NA)
    chosen = jnp.where(inside, ahead, atom_ids[:, None] - direction * stride)
    return jnp.concatenate([partner[:, None], distant[:, None], chosen], axis=1).astype(jnp.int32)


def draw_phonon_shift(key, part):
    key_values, key_order = jax.random.split(jax.random.fold_in(key, 23))
    others = jax.random.randint(key_values, (Q - 2,), 1, SHIFT_MAX + 1, dtype=jnp.int32)
    fixed_ends = jnp.array([SHIFT_MAX, 1], dtype=jnp.int32)
    joined = jnp.concatenate([fixed_ends, others]).astype(jnp.int32)
    return jax.random.permutation(key_order, joined).astype(jnp.int32)


def level_of(stream_key, extent, pieces, low, largest):
    gain, own = 1.0, jax.random.fold_in(stream_key, 6)
    for dim, shards_of in pieces:
        steps = jnp.exp(jax.random.uniform(jax.random.fold_in(own, dim), (shards_of,), jnp.float32, low / len(pieces), largest / len(pieces)))
        gain = gain * jnp.repeat(steps, extent[dim] // shards_of).reshape([-1 if axis == dim else 1 for axis in range(len(extent))])
    return gain


def normal_values(key, extent, spread, limit, pieces=(), held_as=jnp.bfloat16):
    drawn = spread * jax.random.normal(key, extent, jnp.float32)
    if pieces:
        drawn = drawn * level_of(key, extent, pieces, -0.22, 0.18)
    return jnp.clip(drawn, -limit, limit).astype(held_as)


def setup_inputs(seed: int = 0) -> dict:
    arg_keys = jax.random.split(jax.random.key(seed), 7)
    return {
        "green": normal_values(arg_keys[0], (NE, 2, N, N), ((2 * N) ** -0.25), 0.75, ((0, 32), (2, 8)), jnp.float32),
        "sigma": normal_values(arg_keys[1], (NE, N // BS, 2, BS, BS), (2 * BS) ** -0.5, 0.375, ((0, 32), (1, 8)), jnp.float32),
        "neighbours": draw_neighbours(jax.random.fold_in(arg_keys[6], 71), 0),
        "phonon_shift": draw_phonon_shift(jax.random.fold_in(arg_keys[6], 71), 0),
        "phonon_weight": jnp.clip(jnp.exp(jax.random.uniform(arg_keys[4], (2, Q), jnp.float32, math.log(0.1), math.log(0.6))), 0.1, 0.6),
        "dham": normal_values(arg_keys[5], (PAIRS, 3, W, W), W ** -0.5, 2.0, ((0, 8),), jnp.float32),
    }


HIGHEST = lax.Precision.HIGHEST


def multiply(left, right, form):
    return jnp.einsum(form, left, right, precision=HIGHEST)


def self_energy_product(green_energy, sigma_energy):
    row_count = green_energy.shape[1]
    block_count = sigma_energy.shape[0]
    columns = green_energy.reshape(2, row_count, block_count, BS)
    form = 'rmi,mij->rmj'
    real_part = multiply(columns[0], sigma_energy[:, 0], form) - multiply(columns[1], sigma_energy[:, 1], form)
    imag_part = multiply(columns[0], sigma_energy[:, 1], form) + multiply(columns[1], sigma_energy[:, 0], form)
    return jnp.stack([real_part, imag_part]).reshape(2, row_count, block_count * BS)


def lesser_blocks(green_energy, product, neighbours):
    offsets = jnp.arange(W, dtype=jnp.int32)

    def one_atom(atom):
        mine = lax.dynamic_slice_in_dim(product, atom * W, W, 1)
        wanted = (neighbours[atom][:, None] * W + offsets[None, :]).reshape(-1).astype(jnp.int32)
        nearby = jnp.take(green_energy, wanted, axis=1)
        form = 'wn,vn->wv'
        real_part = multiply(mine[0], nearby[0], form) + multiply(mine[1], nearby[1], form)
        imag_part = multiply(mine[1], nearby[0], form) - multiply(mine[0], nearby[1], form)
        block = jnp.stack([real_part, imag_part]).reshape(2, W, K, W).transpose(2, 0, 1, 3)
        return block.reshape(K, 2 * W * W)

    return lax.map(one_atom, jnp.arange(NA, dtype=jnp.int32)).reshape(NA * K, 2 * W * W)


def build_kernel(phonon_shift, phonon_weight, energies):
    rows_e = jnp.arange(energies, dtype=jnp.int32)[None, :, None]
    cols_f = jnp.arange(energies, dtype=jnp.int32)[None, None, :]
    shifts = phonon_shift[:, None, None]
    emission = (cols_f == rows_e + shifts).astype(jnp.float32)
    absorption = (cols_f == rows_e - shifts).astype(jnp.float32)
    terms = phonon_weight[0][:, None, None] * emission + phonon_weight[1][:, None, None] * absorption
    return jnp.sum(terms, axis=0)


def scatter_blocks(smeared, dham):
    energies, pair_count = smeared.shape[0], smeared.shape[1]
    split = smeared.reshape(energies, pair_count, 2, W, W)
    halfway = jnp.einsum('pcij,epzjk->epczik', dham, split, precision=HIGHEST)
    result = jnp.einsum('epczik,pclk->epzil', halfway, dham, precision=HIGHEST)
    return result.reshape(energies, pair_count, 2 * W * W)


def reference(green, sigma, neighbours, phonon_shift, phonon_weight, dham):
    def per_energy(index):
        green_energy = green[index]
        product = self_energy_product(green_energy, sigma[index])
        return lesser_blocks(green_energy, product, neighbours)

    lesser = lax.map(per_energy, jnp.arange(NE, dtype=jnp.int32))
    kernel = build_kernel(phonon_shift, phonon_weight, NE)
    smeared = jnp.einsum('ef,fpx->epx', kernel, lesser, precision=HIGHEST)
    return scatter_blocks(smeared, dham)
```

```python
import functools

import jax
import jax.numpy as jnp
from jax import lax
from jax.experimental import pallas as pl
from jax.experimental.pallas import tpu as pltpu
from jax.sharding import PartitionSpec as P

W = 8
BS = 128
HALO = 32
LEVELS = 8
MESH = pl.DeviceIdType.MESH
HIGHEST = lax.Precision.HIGHEST
F32 = jnp.float32
BF16 = jnp.bfloat16


def split(x):
    high = x.astype(BF16)
    return high, (x - high.astype(F32)).astype(BF16)


def dot(a, b):
    return jnp.dot(a, b, preferred_element_type=F32)


def dot_nt(a, b):
    return lax.dot_general(a, b, (((1,), (1,)), ((), ())), preferred_element_type=F32)


def iota(shape, dim):
    return lax.broadcasted_iota(jnp.int32, shape, dim)


def main_kernel(
    ne, green, sigma, slab, nbt, shift, weight, out,
    ext, sig, acc, bx, xin, rcv, smeared, half, done, slab_v, nbt_v, zed, dlane, bd, kmat,
    loc_sem, sig_send, sig_recv, halo_send, halo_recv, x_send, x_recv,
    a_send, a_recv, b_send, b_recv,
):
    en = lax.axis_index("energy")
    me = lax.axis_index("orb")
    up = lax.rem(me + 1, LEVELS)
    down = lax.rem(me + LEVELS - 1, LEVELS)
    rows = green.shape[1]
    half_rows = rows // 2 + HALO

    barrier = pltpu.get_barrier_semaphore()
    for z in (up, down):
        pl.semaphore_signal(barrier, inc=1, device_id=(en, z), device_id_type=MESH)

    def greet(d, carry):
        pl.semaphore_signal(
            barrier, inc=1, device_id=(lax.rem(en + d, ne), me), device_id_type=MESH
        )
        return carry

    lax.fori_loop(1, ne, greet, 0)

    own_green = pltpu.make_async_copy(green, ext.at[:, pl.ds(HALO, rows), :], loc_sem.at[0])
    own_sigma = pltpu.make_async_copy(sigma, sig.at[pl.ds(2 * me, 2)], loc_sem.at[1])
    own_slab = pltpu.make_async_copy(slab, slab_v, loc_sem.at[2])
    own_nbt = pltpu.make_async_copy(nbt, nbt_v, loc_sem.at[3])
    own_slab.start()
    own_nbt.start()
    own_sigma.start()
    own_green.start()
    pl.semaphore_wait(barrier, ne + 1)

    def at_up(dev, t):
        return 2 * lax.rem(dev - t + 2 * LEVELS, LEVELS)

    def at_down(dev, t):
        return 2 * lax.rem(dev + t, LEVELS) + 1

    def sig_up(t, src=None):
        m = at_up(up, t)
        return pltpu.make_async_remote_copy(
            src_ref=sig.at[m] if src is None else src, dst_ref=sig.at[m],
            send_sem=sig_send.at[0, t], recv_sem=sig_recv.at[0, t],
            device_id=(en, up), device_id_type=MESH,
        )

    def sig_down(t, src=None):
        m = at_down(down, t)
        return pltpu.make_async_remote_copy(
            src_ref=sig.at[m] if src is None else src, dst_ref=sig.at[m],
            send_sem=sig_send.at[1, t], recv_sem=sig_recv.at[1, t],
            device_id=(en, down), device_id_type=MESH,
        )

    def columns(m):
        return pl.ds(pl.multiple_of(m * BS, BS), BS)

    def halo(t):
        copies = []
        for side, (dev, src_row, dst_row) in enumerate(
            ((up, rows - HALO, 0), (down, 0, rows + HALO))
        ):
            for which, m in enumerate((at_up(dev, t), at_down(dev, t))):
                copies.append(
                    pltpu.make_async_remote_copy(
                        src_ref=green.at[:, pl.ds(src_row, HALO), columns(m)],
                        dst_ref=ext.at[:, pl.ds(dst_row, HALO), columns(m)],
                        send_sem=halo_send.at[2 * side + which, t],
                        recv_sem=halo_recv.at[2 * side + which, t],
                        device_id=(en, dev), device_id_type=MESH,
                    )
                )
        return copies

    sig_up(1, sigma.at[0]).start()
    sig_down(1, sigma.at[1]).start()
    for copy in halo(0) + halo(1):
        copy.start()

    own_slab.wait()
    own_nbt.wait()
    pairs = slab.shape[1]
    degree = nbt.shape[0]
    pick = (iota((pairs, BS), 0) == en * degree + iota((pairs, BS), 1) // W).astype(F32)
    zed[...] = jnp.dot(slab_v[...], pick, preferred_element_type=F32, precision=HIGHEST)
    for c in range(3):
        for j in range(W):
            dlane[c * W + j] = zed[pl.ds(c * 64 + j, W, stride=W), :]
    atoms = rows // W
    near = jnp.where(iota((degree, atoms), 1) == en, nbt_v[...].astype(F32), 0.0)
    near = jnp.sum(near, axis=1, keepdims=True)
    off = jnp.where(
        iota((degree, BS), 0) == iota((degree, BS), 1) // W,
        jnp.broadcast_to(near, (degree, BS)), 0.0,
    )
    off = jnp.sum(off, axis=0, keepdims=True) - (me * atoms + en).astype(F32)
    place = off + 8.0 - (off > 0.0).astype(F32)
    place = jnp.broadcast_to(place, (W, BS))
    lane_l = iota((W, BS), 1) % W
    for c in range(3):
        v = jnp.zeros((W, BS), F32)
        for i in range(W):
            v = jnp.where(lane_l == i, zed[pl.ds(c * 64 + i * W, W), :], v)
        for d in range(2 * W):
            bd[pl.ds(d * W, W), pl.ds(c * BS, BS)] = jnp.where(place == float(d), v, 0.0)
    delta = iota((ne, ne), 1) - iota((ne, ne), 0)
    k = jnp.zeros((ne, ne), F32)
    for q in range(shift.shape[0]):
        k = k + jnp.where(delta == shift[q], weight[0, q], 0.0)
        k = k + jnp.where(delta == -shift[q], weight[1, q], 0.0)
    kmat[...] = k

    acc[...] = jnp.zeros_like(acc)
    own_sigma.wait()
    own_green.wait()

    def block(m):
        cols = columns(m)
        x = jnp.concatenate([ext[0, :, cols], ext[1, :, cols]], axis=1)
        xh, xl = split(x)
        sr, si = sig[m, 0], sig[m, 1]
        w = jnp.concatenate(
            [jnp.concatenate([sr, si], axis=1), jnp.concatenate([-si, sr], axis=1)], axis=0
        )
        wh, wl = split(w)
        ph, pq = split(dot(xh, wh) + (dot(xh, wl) + dot(xl, wh)))

        def stacked(v):
            return jnp.concatenate(
                [v, jnp.concatenate([v[:, BS:], -v[:, :BS]], axis=1)], axis=0
            )

        for h in range(2):
            lo, c0 = h * half_rows, h * 2 * HALO
            lh = stacked(ph[lo:lo + half_rows])
            lq = stacked(pq[lo:lo + half_rows])
            bh, bq = xh[c0:c0 + 256], xl[c0:c0 + 256]
            acc[h] += dot_nt(lh, bh) + (dot_nt(lh, bq) + dot_nt(lq, bh))

    def step(t, carry):
        @pl.when(t > 0)
        def _():
            sig_up(t).wait_recv()
            sig_down(t).wait_recv()

        @pl.when((t > 0) & (t < LEVELS - 1))
        def _():
            sig_up(t + 1).start()
            sig_down(t + 1).start()
            for copy in halo(t + 1):
                copy.start()

        for copy in halo(t):
            copy.wait_recv()
        first, second = at_up(me, t), at_down(me, t)

        def inner(u, c):
            block(first + u * (second - first))
            return c

        lax.fori_loop(0, 2, inner, 0)
        return carry

    lax.fori_loop(0, LEVELS, step, 0)

    lane = iota((W, BS), 1)

    def extract(h, i):
        s = ((64 if h == 0 else 224) - 8 * i) % 256
        s2 = (s - 8) % 256
        for z in range(2):
            x = acc[h, pl.ds(z * half_rows + 8 * i, W), :]
            y1 = pltpu.roll(x, s, 1)[:, :BS] if s else x[:, :BS]
            y2 = pltpu.roll(x, s2, 1)[:, :BS] if s2 else x[:, :BS]
            bx[h * 20 + i, pl.ds(z * W, W), :] = jnp.where(lane < 64, y1, y2)

    for i in range(4):
        extract(0, i)
        extract(1, 16 + i)
    to_down = pltpu.make_async_remote_copy(
        src_ref=bx.at[pl.ds(0, 4)], dst_ref=xin.at[1],
        send_sem=x_send.at[1], recv_sem=x_recv.at[1],
        device_id=(en, down), device_id_type=MESH,
    )
    to_up = pltpu.make_async_remote_copy(
        src_ref=bx.at[pl.ds(atoms + 4, 4)], dst_ref=xin.at[0],
        send_sem=x_send.at[0], recv_sem=x_recv.at[0],
        device_id=(en, up), device_id_type=MESH,
    )
    to_down.start()
    to_up.start()
    for i in range(16):
        extract(0, 4 + i)
        extract(1, i)
    to_down.wait_recv()
    to_up.wait_recv()
    lane2 = iota((2 * W, BS), 1)
    for a in range(4):
        bx[4 + a] = jnp.where(lane2 < 8 * (4 - a), xin[0, a], bx[4 + a])
        last = atoms + a
        bx[last] = jnp.where(lane2 >= 64 + 8 * (7 - a), xin[1, a], bx[last])

    own_rows = pl.ds(pl.multiple_of(en * 16, 16), 16)

    def there(d):
        return lax.rem(en + d, ne)

    def back(d):
        return lax.rem(en + ne - d, ne)

    def spread(d):
        to = there(d)
        return pltpu.make_async_remote_copy(
            src_ref=bx.at[4 + to], dst_ref=rcv.at[own_rows, :],
            send_sem=a_send.at[d], recv_sem=a_recv.at[d],
            device_id=(to, me), device_id_type=MESH,
        )

    def arrive(d):
        source = pl.ds(pl.multiple_of(back(d) * 16, 16), 16)
        return pltpu.make_async_remote_copy(
            src_ref=bx.at[4 + there(d)], dst_ref=rcv.at[source, :],
            send_sem=a_send.at[d], recv_sem=a_recv.at[d],
            device_id=(there(d), me), device_id_type=MESH,
        )

    def start_spread(d, carry):
        spread(d).start()
        return carry

    lax.fori_loop(1, ne, start_spread, 0)
    rcv[own_rows, :] = bx[4 + en]

    def wait_spread(d, carry):
        arrive(d).wait_recv()
        return carry

    lax.fori_loop(1, ne, wait_spread, 0)

    xs = jnp.concatenate([rcv[pl.ds(r, ne, stride=16), :] for r in range(16)], axis=1)
    ys = jnp.dot(kmat[...], xs, preferred_element_type=F32, precision=HIGHEST)
    for r in range(16):
        smeared[pl.ds(r, ne, stride=16), :] = ys[:, r * BS:(r + 1) * BS]
    bh, bq = split(bd[...])
    sh, sq = split(smeared[...])
    half[...] = dot(sh, bh) + (dot(sh, bq) + dot(sq, bh))

    def conjugate(e, carry):
        for z in range(2):
            base = pl.multiple_of(e * 16 + z * 8, 8)
            total = jnp.zeros((W, BS), F32)
            for c in range(3):
                block_t = half[pl.ds(base, W), pl.ds(c * BS, BS)]
                for j in range(W):
                    row = jnp.broadcast_to(block_t[j:j + 1, :], (W, BS))
                    total = total + dlane[c * W + j] * row
            done[pl.ds(base, W), :] = total
        return carry

    lax.fori_loop(0, ne, conjugate, 0, unroll=2)

    def back_home(d):
        to = there(d)
        return pltpu.make_async_remote_copy(
            src_ref=done.at[pl.ds(pl.multiple_of(to * 16, 16), 16), :],
            dst_ref=out.at[own_rows, :],
            send_sem=b_send.at[d], recv_sem=b_recv.at[d],
            device_id=(to, me), device_id_type=MESH,
        )

    def home_arrive(d):
        source = pl.ds(pl.multiple_of(back(d) * 16, 16), 16)
        return pltpu.make_async_remote_copy(
            src_ref=done.at[pl.ds(pl.multiple_of(there(d) * 16, 16), 16), :],
            dst_ref=out.at[source, :],
            send_sem=b_send.at[d], recv_sem=b_recv.at[d],
            device_id=(there(d), me), device_id_type=MESH,
        )

    def start_home(d, carry):
        back_home(d).start()
        return carry

    lax.fori_loop(1, ne, start_home, 0)
    keep = pltpu.make_async_copy(done.at[own_rows, :], out.at[own_rows, :], loc_sem.at[0])
    keep.start()

    to_down.wait_send()
    to_up.wait_send()

    def drain_ring(t, carry):
        sig_up(t).wait_send()
        sig_down(t).wait_send()
        return carry

    lax.fori_loop(1, LEVELS, drain_ring, 0)

    def drain_halo(t, carry):
        for copy in halo(t):
            copy.wait_send()
        return carry

    lax.fori_loop(0, LEVELS, drain_halo, 0)

    def finish(d, carry):
        spread(d).wait_send()
        home_arrive(d).wait_recv()
        back_home(d).wait_send()
        return carry

    lax.fori_loop(1, ne, finish, 0)
    keep.wait()


def order_kernel(x_ref, o_ref):
    n = 64
    row, blk = iota((n, BS), 0) % 16, iota((n, BS), 1) // W

    def chunk(c, carry):
        x = x_ref[pl.ds(pl.multiple_of(c * n, n), n), :]
        for b in (1, 2, 4, 8):
            rb, lb = (row // b) % 2, (blk // b) % 2
            upward = pltpu.roll(pltpu.roll(x, n - b, 0), W * b, 1)
            downward = pltpu.roll(pltpu.roll(x, b, 0), BS - W * b, 1)
            x = jnp.where(rb == lb, x, jnp.where(rb == 0, upward, downward))
        o_ref[pl.ds(pl.multiple_of(c * n, n), n), :] = x
        return carry

    lax.fori_loop(0, x_ref.shape[0] // n, chunk, 0)


def per_device(green, sigma, neighbours, phonon_shift, phonon_weight, dham):
    ne = lax.axis_size("energy")
    rows, cols = green.shape[2], green.shape[3]
    atoms, degree = neighbours.shape
    pairs = atoms * degree
    half_rows = rows // 2 + HALO
    slab = dham.transpose(1, 2, 3, 0).reshape(192, pairs)
    anyspec = pl.BlockSpec(memory_space=pl.ANY)
    smem = pl.BlockSpec(memory_space=pltpu.SMEM)
    dma = pltpu.SemaphoreType.DMA
    banded = pl.pallas_call(
        functools.partial(main_kernel, ne),
        out_shape=jax.ShapeDtypeStruct((pairs, BS), F32),
        in_specs=[anyspec, anyspec, anyspec, anyspec, smem, smem],
        out_specs=anyspec,
        scratch_shapes=[
            pltpu.VMEM((2, rows + 2 * HALO, cols), F32),
            pltpu.VMEM((cols // BS, 2, BS, BS), F32),
            pltpu.VMEM((2, 2 * half_rows, 256), F32),
            pltpu.VMEM((atoms + 8, 2 * W, BS), F32),
            pltpu.VMEM((2, 4, 2 * W, BS), F32),
            pltpu.VMEM((ne * 16, BS), F32),
            pltpu.VMEM((ne * 16, BS), F32),
            pltpu.VMEM((ne * 16, 3 * BS), F32),
            pltpu.VMEM((ne * 16, BS), F32),
            pltpu.VMEM((192, pairs), F32),
            pltpu.VMEM((degree, atoms), jnp.int32),
            pltpu.VMEM((192, BS), F32),
            pltpu.VMEM((24, W, BS), F32),
            pltpu.VMEM((BS, 3 * BS), F32),
            pltpu.VMEM((ne, ne), F32),
            dma((4,)),
            dma((2, LEVELS)), dma((2, LEVELS)),
            dma((4, LEVELS)), dma((4, LEVELS)),
            dma((2,)), dma((2,)),
            dma((ne,)), dma((ne,)),
            dma((ne,)), dma((ne,)),
        ],
        compiler_params=pltpu.CompilerParams(
            collective_id=0, has_side_effects=True, vmem_limit_bytes=64_000_000
        ),
        name="lesser",
    )(green[0], sigma[0], slab, neighbours.T, phonon_shift, phonon_weight)
    result = pl.pallas_call(
        order_kernel,
        out_shape=jax.ShapeDtypeStruct((pairs, BS), F32),
        in_specs=[pl.BlockSpec(memory_space=pltpu.VMEM)],
        out_specs=pl.BlockSpec(memory_space=pltpu.VMEM),
        name="order",
    )(banded)
    return result[None]


def solution(mesh):
    return jax.shard_map(
        per_device,
        mesh=mesh,
        in_specs=(
            P("energy", None, "orb", None),
            P("energy", "orb", None, None, None),
            P("orb", None),
            P(),
            P(),
            P("orb", None, None, None),
        ),
        out_specs=P("energy", "orb", None),
        check_vma=False,
    )
```

```python
import functools

import jax
import jax.numpy as jnp
from jax import lax
from jax.experimental import pallas as pl
from jax.experimental.pallas import tpu as pltpu
from jax.sharding import PartitionSpec as P

W = 8
BS = 128
HALO = 32
LEVELS = 8
MESH = pl.DeviceIdType.MESH
HIGHEST = lax.Precision.HIGHEST
F32 = jnp.float32
BF16 = jnp.bfloat16


def split(x):
    high = x.astype(BF16)
    return high, (x - high.astype(F32)).astype(BF16)


def dot(a, b):
    return jnp.dot(a, b, preferred_element_type=F32)


def dot_nt(a, b):
    return lax.dot_general(a, b, (((1,), (1,)), ((), ())), preferred_element_type=F32)


def iota(shape, dim):
    return lax.broadcasted_iota(jnp.int32, shape, dim)


def main_kernel(
    ne, green, sigma, slab, nbt, shift, weight, out,
    ext, sig, acc, bx, xin, rcv, half, done, slab_v, nbt_v, zed, bd, kmat,
    loc_sem, sig_send, sig_recv, halo_send, halo_recv, x_send, x_recv,
    a_send, a_recv, b_send, b_recv,
):
    en = lax.axis_index("energy")
    me = lax.axis_index("orb")
    up = lax.rem(me + 1, LEVELS)
    down = lax.rem(me + LEVELS - 1, LEVELS)
    rows = green.shape[1]
    half_rows = rows // 2 + HALO

    barrier = pltpu.get_barrier_semaphore()
    for z in (up, down):
        pl.semaphore_signal(barrier, inc=1, device_id=(en, z), device_id_type=MESH)

    def greet(d, carry):
        pl.semaphore_signal(
            barrier, inc=1, device_id=(lax.rem(en + d, ne), me), device_id_type=MESH
        )
        return carry

    lax.fori_loop(1, ne, greet, 0)

    own_green = pltpu.make_async_copy(green, ext.at[:, pl.ds(HALO, rows), :], loc_sem.at[0])
    own_sigma = pltpu.make_async_copy(sigma, sig.at[pl.ds(2 * me, 2)], loc_sem.at[1])
    own_slab = pltpu.make_async_copy(slab, slab_v, loc_sem.at[2])
    own_nbt = pltpu.make_async_copy(nbt, nbt_v, loc_sem.at[3])
    own_slab.start()
    own_nbt.start()
    own_sigma.start()
    own_green.start()
    own_slab.wait()
    own_nbt.wait()
    pairs = slab.shape[1]
    degree = nbt.shape[0]
    pick = (iota((pairs, BS), 0) == en * degree + iota((pairs, BS), 1) // W).astype(F32)
    zed[...] = jnp.dot(slab_v[...], pick, preferred_element_type=F32, precision=HIGHEST)
    atoms = rows // W
    near = jnp.where(iota((degree, atoms), 1) == en, nbt_v[...].astype(F32), 0.0)
    near = jnp.sum(near, axis=1, keepdims=True)
    off = jnp.where(
        iota((degree, BS), 0) == iota((degree, BS), 1) // W,
        jnp.broadcast_to(near, (degree, BS)), 0.0,
    )
    off = jnp.sum(off, axis=0, keepdims=True) - (me * atoms + en).astype(F32)
    place = off + 8.0 - (off > 0.0).astype(F32)
    place = jnp.broadcast_to(place, (W, BS))
    lane_l = iota((W, BS), 1) % W
    for c in range(3):
        v = jnp.zeros((W, BS), F32)
        for i in range(W):
            v = jnp.where(lane_l == i, zed[pl.ds(c * 64 + i * W, W), :], v)
        for d in range(2 * W):
            bd[pl.ds(d * W, W), pl.ds(c * BS, BS)] = jnp.where(place == float(d), v, 0.0)
    delta = iota((ne, ne), 1) - iota((ne, ne), 0)
    k = jnp.zeros((ne, ne), F32)
    for q in range(shift.shape[0]):
        k = k + jnp.where(delta == shift[q], weight[0, q], 0.0)
        k = k + jnp.where(delta == -shift[q], weight[1, q], 0.0)
    kmat[...] = k
    acc[...] = jnp.zeros_like(acc)
    pl.semaphore_wait(barrier, ne + 1)

    def at_up(dev, t):
        return 2 * lax.rem(dev - t + 2 * LEVELS, LEVELS)

    def at_down(dev, t):
        return 2 * lax.rem(dev + t, LEVELS) + 1

    def ring(side, t, c, src=None):
        dev = down if side else up
        m = (at_down if side else at_up)(dev, t)
        return pltpu.make_async_remote_copy(
            src_ref=sig.at[m, c] if src is None else src, dst_ref=sig.at[m, c],
            send_sem=sig_send.at[2 * side + c, t], recv_sem=sig_recv.at[2 * side + c, t],
            device_id=(en, dev), device_id_type=MESH,
        )

    def columns(m):
        return pl.ds(pl.multiple_of(m * BS, BS), BS)

    def halo(side, t, c):
        dev, src_row, dst_row = ((up, rows - HALO, 0), (down, 0, rows + HALO))[side]
        m = (at_down if c else at_up)(dev, t)
        return pltpu.make_async_remote_copy(
            src_ref=green.at[:, pl.ds(src_row, HALO), columns(m)],
            dst_ref=ext.at[:, pl.ds(dst_row, HALO), columns(m)],
            send_sem=halo_send.at[2 * side + c, t], recv_sem=halo_recv.at[2 * side + c, t],
            device_id=(en, dev), device_id_type=MESH,
        )

    for c in range(2):
        for side in range(2):
            ring(side, 1, c, sigma.at[side, c]).start()
    for t in range(2):
        for c in range(2):
            for side in range(2):
                halo(side, t, c).start()

    own_sigma.wait()
    own_green.wait()

    def block(m):
        cols = columns(m)
        x = jnp.concatenate([ext[0, :, cols], ext[1, :, cols]], axis=1)
        xh, xl = split(x)
        sr, si = sig[m, 0], sig[m, 1]
        w = jnp.concatenate(
            [jnp.concatenate([sr, si], axis=1), jnp.concatenate([-si, sr], axis=1)], axis=0
        )
        wh, wl = split(w)
        ph, pq = split(dot(xh, wh) + (dot(xh, wl) + dot(xl, wh)))

        def stacked(v):
            return jnp.concatenate(
                [v, jnp.concatenate([v[:, BS:], -v[:, :BS]], axis=1)], axis=0
            )

        for h in range(2):
            lo, c0 = h * half_rows, h * 2 * HALO
            lh = stacked(ph[lo:lo + half_rows])
            lq = stacked(pq[lo:lo + half_rows])
            bh, bq = xh[c0:c0 + 256], xl[c0:c0 + 256]
            acc[h] += dot_nt(lh, bh) + (dot_nt(lh, bq) + dot_nt(lq, bh))

    def step(t, carry):
        for c in range(2):
            for side in range(2):
                @pl.when(t < LEVELS)
                def _():
                    ring(side, t, c).wait_recv()

                @pl.when(t < LEVELS - 1)
                def _():
                    ring(side, t + 1, c).start()

            @pl.when(t < LEVELS - 1)
            def _():
                for side in range(2):
                    halo(side, t + 1, c).start()

            for side in range(2):
                halo(side, t - 1, c).wait_recv()
            block((at_down if c else at_up)(me, t - 1))
        return carry

    lax.fori_loop(1, LEVELS + 1, step, 0)

    lane = iota((W, BS), 1)

    def extract(h, i):
        s = ((64 if h == 0 else 224) - 8 * i) % 256
        s2 = (s - 8) % 256
        for z in range(2):
            x = acc[h, pl.ds(z * half_rows + 8 * i, W), :]
            y1 = pltpu.roll(x, s, 1)[:, :BS] if s else x[:, :BS]
            y2 = pltpu.roll(x, s2, 1)[:, :BS] if s2 else x[:, :BS]
            bx[h * 20 + i, pl.ds(z * W, W), :] = jnp.where(lane < 64, y1, y2)

    for i in range(4):
        extract(0, i)
        extract(1, 16 + i)
    to_down = pltpu.make_async_remote_copy(
        src_ref=bx.at[pl.ds(0, 4)], dst_ref=xin.at[1],
        send_sem=x_send.at[1], recv_sem=x_recv.at[1],
        device_id=(en, down), device_id_type=MESH,
    )
    to_up = pltpu.make_async_remote_copy(
        src_ref=bx.at[pl.ds(atoms + 4, 4)], dst_ref=xin.at[0],
        send_sem=x_send.at[0], recv_sem=x_recv.at[0],
        device_id=(en, up), device_id_type=MESH,
    )
    to_down.start()
    to_up.start()
    for i in range(16):
        extract(0, 4 + i)
        extract(1, i)

    own_rows = pl.ds(pl.multiple_of(en * 16, 16), 16)

    def there(d):
        return lax.rem(en + d, ne)

    def back(d):
        return lax.rem(en + ne - d, ne)

    def spread(d):
        to = there(d)
        return pltpu.make_async_remote_copy(
            src_ref=bx.at[4 + to], dst_ref=rcv.at[own_rows, :],
            send_sem=a_send.at[d], recv_sem=a_recv.at[d],
            device_id=(to, me), device_id_type=MESH,
        )

    def arrive(d):
        source = pl.ds(pl.multiple_of(back(d) * 16, 16), 16)
        return pltpu.make_async_remote_copy(
            src_ref=bx.at[4 + there(d)], dst_ref=rcv.at[source, :],
            send_sem=a_send.at[d], recv_sem=a_recv.at[d],
            device_id=(there(d), me), device_id_type=MESH,
        )

    def start_spread(edge):
        def one(d, carry):
            to = there(d)
            at_edge = (to < 4) | (to >= atoms - 4)

            @pl.when(at_edge if edge else jnp.logical_not(at_edge))
            def _():
                spread(d).start()

            return carry

        lax.fori_loop(1, ne, one, 0)

    start_spread(False)
    to_down.wait_recv()
    to_up.wait_recv()
    lane2 = iota((2 * W, BS), 1)
    for a in range(4):
        bx[4 + a] = jnp.where(lane2 < 8 * (4 - a), xin[0, a], bx[4 + a])
        last = atoms + a
        bx[last] = jnp.where(lane2 >= 64 + 8 * (7 - a), xin[1, a], bx[last])
    start_spread(True)
    rcv[own_rows, :] = bx[4 + en]

    def wait_spread(d, carry):
        arrive(d).wait_recv()
        return carry

    lax.fori_loop(1, ne, wait_spread, 0)

    xs = jnp.concatenate([rcv[pl.ds(r, ne, stride=16), :] for r in range(16)], axis=1)
    ys = jnp.dot(kmat[...], xs, preferred_element_type=F32, precision=HIGHEST)
    yh, yq = split(jnp.concatenate([ys[:, r * BS:(r + 1) * BS] for r in range(16)], axis=0))
    bh, bq = split(bd[...])
    half[...] = dot(yh, bh) + (dot(yh, bq) + dot(yq, bh))

    def conjugate(tile, carry):
        v = []
        for z in range(2):
            t = [
                half[
                    pl.ds(pl.multiple_of((z * W + j) * ne + tile * W, W), W),
                    pl.ds(c * BS, BS),
                ]
                for c in range(3) for j in range(W)
            ]
            for i in range(W):
                total = jnp.zeros((W, BS), F32)
                for c in range(3):
                    for j in range(W):
                        row = jnp.broadcast_to(zed[pl.ds(c * 64 + i * W + j, 1), :], (W, BS))
                        total = total + row * t[c * W + j]
                v.append(total)
        for b in (1, 2, 4, 8):
            keep_low = (lane // (W * b)) % 2 == 0
            new = list(v)
            for r in range(16):
                if not r & b:
                    new[r] = jnp.where(keep_low, v[r], pltpu.roll(v[r + b], W * b, 1))
                    new[r + b] = jnp.where(keep_low, pltpu.roll(v[r], BS - W * b, 1), v[r + b])
            v = new
        for k in range(16):
            done[pl.ds(tile * BS + k, W, stride=16), :] = v[k]
        return carry

    lax.fori_loop(0, ne // W, conjugate, 0)

    def back_home(d):
        to = there(d)
        return pltpu.make_async_remote_copy(
            src_ref=done.at[pl.ds(pl.multiple_of(to * 16, 16), 16), :],
            dst_ref=out.at[own_rows, :],
            send_sem=b_send.at[d], recv_sem=b_recv.at[d],
            device_id=(to, me), device_id_type=MESH,
        )

    def home_arrive(d):
        source = pl.ds(pl.multiple_of(back(d) * 16, 16), 16)
        return pltpu.make_async_remote_copy(
            src_ref=done.at[pl.ds(pl.multiple_of(there(d) * 16, 16), 16), :],
            dst_ref=out.at[source, :],
            send_sem=b_send.at[d], recv_sem=b_recv.at[d],
            device_id=(there(d), me), device_id_type=MESH,
        )

    def start_home(d, carry):
        back_home(d).start()
        return carry

    lax.fori_loop(1, ne, start_home, 0)
    keep = pltpu.make_async_copy(done.at[own_rows, :], out.at[own_rows, :], loc_sem.at[0])
    keep.start()

    to_down.wait_send()
    to_up.wait_send()

    def drain_ring(t, carry):
        for c in range(2):
            for side in range(2):
                ring(side, t, c).wait_send()
        return carry

    lax.fori_loop(1, LEVELS, drain_ring, 0)

    def drain_halo(t, carry):
        for c in range(2):
            for side in range(2):
                halo(side, t, c).wait_send()
        return carry

    lax.fori_loop(0, LEVELS, drain_halo, 0)

    def finish(d, carry):
        spread(d).wait_send()
        home_arrive(d).wait_recv()
        back_home(d).wait_send()
        return carry

    lax.fori_loop(1, ne, finish, 0)
    keep.wait()


def per_device(green, sigma, neighbours, phonon_shift, phonon_weight, dham):
    ne = lax.axis_size("energy")
    rows, cols = green.shape[2], green.shape[3]
    atoms, degree = neighbours.shape
    pairs = atoms * degree
    half_rows = rows // 2 + HALO
    slab = dham.transpose(1, 2, 3, 0).reshape(192, pairs)
    anyspec = pl.BlockSpec(memory_space=pl.ANY)
    smem = pl.BlockSpec(memory_space=pltpu.SMEM)
    dma = pltpu.SemaphoreType.DMA
    banded = pl.pallas_call(
        functools.partial(main_kernel, ne),
        out_shape=jax.ShapeDtypeStruct((pairs, BS), F32),
        in_specs=[anyspec, anyspec, anyspec, anyspec, smem, smem],
        out_specs=anyspec,
        scratch_shapes=[
            pltpu.VMEM((2, rows + 2 * HALO, cols), F32),
            pltpu.VMEM((cols // BS, 2, BS, BS), F32),
            pltpu.VMEM((2, 2 * half_rows, 256), F32),
            pltpu.VMEM((atoms + 8, 2 * W, BS), F32),
            pltpu.VMEM((2, 4, 2 * W, BS), F32),
            pltpu.VMEM((ne * 16, BS), F32),
            pltpu.VMEM((ne * 16, 3 * BS), F32),
            pltpu.VMEM((ne * 16, BS), F32),
            pltpu.VMEM((192, pairs), F32),
            pltpu.VMEM((degree, atoms), jnp.int32),
            pltpu.VMEM((192, BS), F32),
            pltpu.VMEM((BS, 3 * BS), F32),
            pltpu.VMEM((ne, ne), F32),
            dma((4,)),
            dma((4, LEVELS)), dma((4, LEVELS)),
            dma((4, LEVELS)), dma((4, LEVELS)),
            dma((2,)), dma((2,)),
            dma((ne,)), dma((ne,)),
            dma((ne,)), dma((ne,)),
        ],
        compiler_params=pltpu.CompilerParams(
            collective_id=0, has_side_effects=True, vmem_limit_bytes=64_000_000
        ),
        name="lesser",
    )(green[0], sigma[0], slab, neighbours.T, phonon_shift, phonon_weight)
    return banded[None]


def solution(mesh):
    return jax.shard_map(
        per_device,
        mesh=mesh,
        in_specs=(
            P("energy", None, "orb", None),
            P("energy", "orb", None, None, None),
            P("orb", None),
            P(),
            P(),
            P("orb", None, None, None),
        ),
        out_specs=P("energy", "orb", None),
        check_vma=False,
    )
```

```python
import functools

import jax
import jax.numpy as jnp
from jax import lax
from jax.experimental import pallas as pl
from jax.experimental.pallas import tpu as pltpu
from jax.sharding import PartitionSpec as P

W = 8
BS = 128
HALO = 32
LEVELS = 8
SIDE = 4
MESH = pl.DeviceIdType.MESH
FAR_FIRST = sorted(
    ((dy, dx, dc) for dy in range(SIDE) for dx in range(SIDE) for dc in range(2) if dy or dx or dc),
    key=lambda o: -(min(o[0], SIDE - o[0]) + min(o[1], SIDE - o[1])),
)
HIGHEST = lax.Precision.HIGHEST
F32 = jnp.float32
BF16 = jnp.bfloat16


def split(x):
    high = x.astype(BF16)
    return high, (x - high.astype(F32)).astype(BF16)


def dot(a, b):
    return jnp.dot(a, b, preferred_element_type=F32)


def dot_nt(a, b):
    return lax.dot_general(a, b, (((1,), (1,)), ((), ())), preferred_element_type=F32)


def iota(shape, dim):
    return lax.broadcasted_iota(jnp.int32, shape, dim)


def main_kernel(
    ne, green, sigma, slab, nbt, shift, weight, out,
    ext, sig, acc, bx, xin, rcv, half, done, slab_v, nbt_v, zed, zexp, bd, kmat, known,
    loc_sem, sig_send, sig_recv, halo_send, halo_recv, x_send, x_recv,
    a_send, a_recv, b_send, b_recv,
):
    en = lax.axis_index("energy")
    me = lax.axis_index("orb")
    up = lax.rem(me + 1, LEVELS)
    down = lax.rem(me + LEVELS - 1, LEVELS)
    rows = green.shape[1]
    half_rows = rows // 2 + HALO

    core, chip_x, chip_y = en % 2, en // 2 % SIDE, en // (2 * SIDE)

    def moved(dy, dx, dc):
        return (
            (chip_y + dy + SIDE) % SIDE * SIDE + (chip_x + dx + SIDE) % SIDE
        ) * 2 + (core + dc) % 2

    barrier = pltpu.get_barrier_semaphore()
    for z in (up, down):
        pl.semaphore_signal(barrier, inc=1, device_id=(en, z), device_id_type=MESH)
    for step_to in ((0, 1, 0), (0, -1, 0), (1, 0, 0), (-1, 0, 0), (0, 0, 1)):
        pl.semaphore_signal(
            barrier, inc=1, device_id=(moved(*step_to), me), device_id_type=MESH
        )

    def tell(r):
        for sign in (1, -1):
            to = moved(0, sign, 0) if r < 2 else moved(sign, 0, 0)
            pl.semaphore_signal(known.at[r], inc=1, device_id=(to, me), device_id_type=MESH)

    own_green = pltpu.make_async_copy(green, ext.at[:, pl.ds(HALO, rows), :], loc_sem.at[0])
    own_sigma = pltpu.make_async_copy(sigma, sig.at[pl.ds(2 * me, 2)], loc_sem.at[1])
    own_slab = pltpu.make_async_copy(slab, slab_v, loc_sem.at[2])
    own_nbt = pltpu.make_async_copy(nbt, nbt_v, loc_sem.at[3])
    own_slab.start()
    own_nbt.start()
    own_sigma.start()
    own_green.start()
    pl.semaphore_wait(barrier, 7)

    def at_up(dev, t):
        return 2 * lax.rem(dev - t + 2 * LEVELS, LEVELS)

    def at_down(dev, t):
        return 2 * lax.rem(dev + t, LEVELS) + 1

    def ring(side, t, c, src=None):
        dev = down if side else up
        m = (at_down if side else at_up)(dev, t)
        return pltpu.make_async_remote_copy(
            src_ref=sig.at[m, c] if src is None else src, dst_ref=sig.at[m, c],
            send_sem=sig_send.at[2 * side + c, t], recv_sem=sig_recv.at[2 * side + c, t],
            device_id=(en, dev), device_id_type=MESH,
        )

    def columns(m):
        return pl.ds(pl.multiple_of(m * BS, BS), BS)

    def halo(side, t, c):
        dev, src_row, dst_row = ((up, rows - HALO, 0), (down, 0, rows + HALO))[side]
        m = (at_down if c else at_up)(dev, t)
        return pltpu.make_async_remote_copy(
            src_ref=green.at[:, pl.ds(src_row, HALO), columns(m)],
            dst_ref=ext.at[:, pl.ds(dst_row, HALO), columns(m)],
            send_sem=halo_send.at[2 * side + c, t], recv_sem=halo_recv.at[2 * side + c, t],
            device_id=(en, dev), device_id_type=MESH,
        )

    for c in range(2):
        for side in range(2):
            ring(side, 1, c, sigma.at[side, c]).start()
    for t in range(2):
        for c in range(2):
            for side in range(2):
                halo(side, t, c).start()
    tell(0)

    own_slab.wait()
    own_nbt.wait()
    pairs = slab.shape[1]
    degree = nbt.shape[0]
    pick = (iota((pairs, BS), 0) == en * degree + iota((pairs, BS), 1) // W).astype(F32)
    zed[...] = jnp.dot(slab_v[...], pick, preferred_element_type=F32, precision=HIGHEST)
    atoms = rows // W
    near = jnp.where(iota((degree, atoms), 1) == en, nbt_v[...].astype(F32), 0.0)
    near = jnp.sum(near, axis=1, keepdims=True)
    off = jnp.where(
        iota((degree, BS), 0) == iota((degree, BS), 1) // W,
        jnp.broadcast_to(near, (degree, BS)), 0.0,
    )
    off = jnp.sum(off, axis=0, keepdims=True) - (me * atoms + en).astype(F32)
    place = off + 8.0 - (off > 0.0).astype(F32)
    place = jnp.broadcast_to(place, (W, BS))
    lane_l = iota((W, BS), 1) % W
    for c in range(3):
        v = jnp.zeros((W, BS), F32)
        for i in range(W):
            v = jnp.where(lane_l == i, zed[pl.ds(c * 64 + i * W, W), :], v)
        for d in range(2 * W):
            bd[pl.ds(d * W, W), pl.ds(c * BS, BS)] = jnp.where(place == float(d), v, 0.0)
    delta = iota((ne, ne), 1) - iota((ne, ne), 0)
    k = jnp.zeros((ne, ne), F32)
    for q in range(shift.shape[0]):
        k = k + jnp.where(delta == shift[q], weight[0, q], 0.0)
        k = k + jnp.where(delta == -shift[q], weight[1, q], 0.0)
    kmat[...] = k
    acc[...] = jnp.zeros_like(acc)

    def widen(r, carry):
        tile = zed[pl.ds(pl.multiple_of(r * W, W), W), :]
        for j in range(W):
            zexp[r * W + j] = jnp.broadcast_to(tile[j:j + 1, :], (W, BS))
        return carry

    lax.fori_loop(0, 24, widen, 0)

    own_sigma.wait()
    own_green.wait()

    def block(m):
        cols = columns(m)
        x = jnp.concatenate([ext[0, :, cols], ext[1, :, cols]], axis=1)
        xh, xl = split(x)
        sr, si = sig[m, 0], sig[m, 1]
        w = jnp.concatenate(
            [jnp.concatenate([sr, si], axis=1), jnp.concatenate([-si, sr], axis=1)], axis=0
        )
        wh, wl = split(w)
        ph, pq = split(dot(xh, wh) + (dot(xh, wl) + dot(xl, wh)))

        def stacked(v):
            return jnp.concatenate(
                [v, jnp.concatenate([v[:, BS:], -v[:, :BS]], axis=1)], axis=0
            )

        for h in range(2):
            lo, c0 = h * half_rows, h * 2 * HALO
            lh = stacked(ph[lo:lo + half_rows])
            lq = stacked(pq[lo:lo + half_rows])
            bh, bq = xh[c0:c0 + 256], xl[c0:c0 + 256]
            acc[h] += dot_nt(lh, bh) + (dot_nt(lh, bq) + dot_nt(lq, bh))

    def due(t, c):
        for side in range(2):
            halo(side, t, c).wait_recv()
        block((at_down if c else at_up)(me, t))

    def step(t, carry):
        for c in range(2):
            for side in range(2):
                ring(side, t, c).wait_recv()
                ring(side, t + 1, c).start()
            for side in range(2):
                halo(side, t + 1, c).start()
            due(t - 1, c)
        for r in range(4):
            @pl.when(t == r + 1)
            def _():
                pl.semaphore_wait(known.at[r], 2)
                if r < 3:
                    tell(r + 1)
        return carry

    lax.fori_loop(1, LEVELS - 1, step, 0)

    def last(t, carry):
        @pl.when(t == LEVELS - 1)
        def _():
            for c in range(2):
                for side in range(2):
                    ring(side, t, c).wait_recv()

        due(t, 0)
        due(t, 1)
        return carry

    lax.fori_loop(LEVELS - 2, LEVELS, last, 0)

    lane = iota((W, BS), 1)

    def extract(h, i):
        s = ((64 if h == 0 else 224) - 8 * i) % 256
        s2 = (s - 8) % 256
        for z in range(2):
            x = acc[h, pl.ds(z * half_rows + 8 * i, W), :]
            y1 = pltpu.roll(x, s, 1)[:, :BS] if s else x[:, :BS]
            y2 = pltpu.roll(x, s2, 1)[:, :BS] if s2 else x[:, :BS]
            bx[h * 20 + i, pl.ds(z * W, W), :] = jnp.where(lane < 64, y1, y2)

    for i in range(4):
        extract(0, i)
        extract(1, 16 + i)
    to_down = pltpu.make_async_remote_copy(
        src_ref=bx.at[pl.ds(0, 4)], dst_ref=xin.at[1],
        send_sem=x_send.at[1], recv_sem=x_recv.at[1],
        device_id=(en, down), device_id_type=MESH,
    )
    to_up = pltpu.make_async_remote_copy(
        src_ref=bx.at[pl.ds(atoms + 4, 4)], dst_ref=xin.at[0],
        send_sem=x_send.at[0], recv_sem=x_recv.at[0],
        device_id=(en, up), device_id_type=MESH,
    )
    to_down.start()
    to_up.start()
    for i in range(16):
        extract(0, 4 + i)
        extract(1, i)

    own_rows = pl.ds(pl.multiple_of(en * 16, 16), 16)

    def there(d):
        return moved(*FAR_FIRST[d])

    def back(d):
        dy, dx, dc = FAR_FIRST[d]
        return moved(-dy, -dx, dc)

    def rows_of(e):
        return pl.ds(pl.multiple_of(e * 16, 16), 16)

    def spread(d, source=None):
        to = there(d)
        return pltpu.make_async_remote_copy(
            src_ref=bx.at[4 + to],
            dst_ref=rcv.at[own_rows if source is None else rows_of(source), :],
            send_sem=a_send.at[d], recv_sem=a_recv.at[d],
            device_id=(to, me), device_id_type=MESH,
        )

    def start_spread(edge):
        for d in range(ne - 1):
            to = there(d)
            at_edge = (to < 4) | (to >= atoms - 4)

            @pl.when(at_edge if edge else jnp.logical_not(at_edge))
            def _():
                spread(d).start()

    start_spread(False)
    to_down.wait_recv()
    to_up.wait_recv()
    lane2 = iota((2 * W, BS), 1)
    for a in range(4):
        bx[4 + a] = jnp.where(lane2 < 8 * (4 - a), xin[0, a], bx[4 + a])
        last = atoms + a
        bx[last] = jnp.where(lane2 >= 64 + 8 * (7 - a), xin[1, a], bx[last])
    start_spread(True)
    rcv[own_rows, :] = bx[4 + en]

    for d in range(ne - 1):
        spread(d, back(d)).wait_recv()

    xs = jnp.concatenate([rcv[pl.ds(r, ne, stride=16), :] for r in range(16)], axis=1)
    xh, xq = split(xs)
    kh, kq = split(kmat[...])
    ys = dot(kh, xh) + (dot(kh, xq) + dot(kq, xh))
    yh, yq = split(jnp.concatenate([ys[:, r * BS:(r + 1) * BS] for r in range(16)], axis=0))
    bh, bq = split(bd[...])
    half[...] = dot(yh, bh) + (dot(yh, bq) + dot(yq, bh))

    def conjugate(tile):
        v = []
        for z in range(2):
            t = [
                half[
                    pl.ds((z * W + j) * ne + tile * W, W),
                    pl.ds(c * BS, BS),
                ]
                for c in range(3) for j in range(W)
            ]
            for i in range(W):
                total = [None, None]
                for c in range(3):
                    for j in range(W):
                        term = zexp[c * 64 + i * W + j] * t[c * W + j]
                        total[j % 2] = term if total[j % 2] is None else total[j % 2] + term
                v.append(total[0] + total[1])
        for b in (1, 2, 4, 8):
            keep_low = (lane // (W * b)) % 2 == 0
            new = list(v)
            for r in range(16):
                if not r & b:
                    new[r] = jnp.where(keep_low, v[r], pltpu.roll(v[r + b], W * b, 1))
                    new[r + b] = jnp.where(keep_low, pltpu.roll(v[r], BS - W * b, 1), v[r + b])
            v = new
        for k in range(16):
            done[pl.ds(tile * BS + k, W, stride=16), :] = v[k]

    for tile in range(ne // W):
        conjugate(tile)

    def back_home(d, source=None):
        to = there(d)
        return pltpu.make_async_remote_copy(
            src_ref=done.at[rows_of(to), :],
            dst_ref=out.at[own_rows if source is None else rows_of(source), :],
            send_sem=b_send.at[d], recv_sem=b_recv.at[d],
            device_id=(to, me), device_id_type=MESH,
        )

    for d in range(ne - 1):
        back_home(d).start()
    keep = pltpu.make_async_copy(done.at[own_rows, :], out.at[own_rows, :], loc_sem.at[0])
    keep.start()

    to_down.wait_send()
    to_up.wait_send()

    def drain_ring(t, carry):
        for c in range(2):
            for side in range(2):
                ring(side, t, c).wait_send()
        return carry

    lax.fori_loop(1, LEVELS, drain_ring, 0)

    def drain_halo(t, carry):
        for c in range(2):
            for side in range(2):
                halo(side, t, c).wait_send()
        return carry

    lax.fori_loop(0, LEVELS, drain_halo, 0)

    for d in range(ne - 1):
        spread(d).wait_send()
    for d in range(ne - 1):
        back_home(d, back(d)).wait_recv()
    for d in range(ne - 1):
        back_home(d).wait_send()
    keep.wait()


def per_device(green, sigma, neighbours, phonon_shift, phonon_weight, dham):
    ne = lax.axis_size("energy")
    rows, cols = green.shape[2], green.shape[3]
    atoms, degree = neighbours.shape
    pairs = atoms * degree
    half_rows = rows // 2 + HALO
    slab = dham.transpose(1, 2, 3, 0).reshape(192, pairs)
    anyspec = pl.BlockSpec(memory_space=pl.ANY)
    smem = pl.BlockSpec(memory_space=pltpu.SMEM)
    dma = pltpu.SemaphoreType.DMA
    banded = pl.pallas_call(
        functools.partial(main_kernel, ne),
        out_shape=jax.ShapeDtypeStruct((pairs, BS), F32),
        in_specs=[anyspec, anyspec, anyspec, anyspec, smem, smem],
        out_specs=anyspec,
        scratch_shapes=[
            pltpu.VMEM((2, rows + 2 * HALO, cols), F32),
            pltpu.VMEM((cols // BS, 2, BS, BS), F32),
            pltpu.VMEM((2, 2 * half_rows, 256), F32),
            pltpu.VMEM((atoms + 8, 2 * W, BS), F32),
            pltpu.VMEM((2, 4, 2 * W, BS), F32),
            pltpu.VMEM((ne * 16, BS), F32),
            pltpu.VMEM((ne * 16, 3 * BS), F32),
            pltpu.VMEM((ne * 16, BS), F32),
            pltpu.VMEM((192, pairs), F32),
            pltpu.VMEM((degree, atoms), jnp.int32),
            pltpu.VMEM((192, BS), F32),
            pltpu.VMEM((192, W, BS), F32),
            pltpu.VMEM((BS, 3 * BS), F32),
            pltpu.VMEM((ne, ne), F32),
            pltpu.SemaphoreType.REGULAR((4,)),
            dma((4,)),
            dma((4, LEVELS)), dma((4, LEVELS)),
            dma((4, LEVELS)), dma((4, LEVELS)),
            dma((2,)), dma((2,)),
            dma((ne,)), dma((ne,)),
            dma((ne,)), dma((ne,)),
        ],
        compiler_params=pltpu.CompilerParams(
            collective_id=0, has_side_effects=True, vmem_limit_bytes=64_000_000
        ),
        name="lesser",
    )(green[0], sigma[0], slab, neighbours.T, phonon_shift, phonon_weight)
    return banded[None]


def solution(mesh):
    return jax.shard_map(
        per_device,
        mesh=mesh,
        in_specs=(
            P("energy", None, "orb", None),
            P("energy", "orb", None, None, None),
            P("orb", None),
            P(),
            P(),
            P("orb", None, None, None),
        ),
        out_specs=P("energy", "orb", None),
        check_vma=False,
    )
```

```python
import functools

import jax
import jax.numpy as jnp
from jax import lax
from jax.experimental import pallas as pl
from jax.experimental.pallas import tpu as pltpu
from jax.sharding import PartitionSpec as P

W = 8
BS = 128
HALO = 32
LEVELS = 8
SIDE = 4
MESH = pl.DeviceIdType.MESH
FAR_FIRST = sorted(
    ((dy, dx, dc) for dy in range(SIDE) for dx in range(SIDE) for dc in range(2) if dy or dx or dc),
    key=lambda o: -(min(o[0], SIDE - o[0]) + min(o[1], SIDE - o[1])),
)
HIGHEST = lax.Precision.HIGHEST
F32 = jnp.float32
BF16 = jnp.bfloat16


def atom_of(e):
    return e // 2 + 16 * (e % 2)


def device_of(a):
    return 2 * (a % 16) + a // 16


def split(x):
    high = x.astype(BF16)
    return high, (x - high.astype(F32)).astype(BF16)


def dot(a, b):
    return jnp.dot(a, b, preferred_element_type=F32)


def dot_nt(a, b):
    return lax.dot_general(a, b, (((1,), (1,)), ((), ())), preferred_element_type=F32)


def iota(shape, dim):
    return lax.broadcasted_iota(jnp.int32, shape, dim)


def main_kernel(
    ne, green, sigma, slab, nbt, shift, weight, out,
    ext, sig, acc, bx, pair, rcv, rcv_n, half, done, slab_v, nbt_v, zed, zexp, bd, kmat, known,
    loc_sem, sig_send, sig_recv, halo_send, halo_recv, n_send, n_recv,
    a_send, a_recv, b_send, b_recv,
):
    en = lax.axis_index("energy")
    me = lax.axis_index("orb")
    up = lax.rem(me + 1, LEVELS)
    down = lax.rem(me + LEVELS - 1, LEVELS)
    rows = green.shape[1]
    mine = atom_of(en)
    half_rows = rows // 2 + HALO

    core, chip_x, chip_y = en % 2, en // 2 % SIDE, en // (2 * SIDE)

    def moved(dy, dx, dc):
        return (
            (chip_y + dy + SIDE) % SIDE * SIDE + (chip_x + dx + SIDE) % SIDE
        ) * 2 + (core + dc) % 2

    barrier = pltpu.get_barrier_semaphore()
    for z in (up, down):
        pl.semaphore_signal(barrier, inc=1, device_id=(en, z), device_id_type=MESH)
    for step_to in ((0, 1, 0), (0, -1, 0), (1, 0, 0), (-1, 0, 0), (0, 0, 1)):
        pl.semaphore_signal(
            barrier, inc=1, device_id=(moved(*step_to), me), device_id_type=MESH
        )

    def tell(r):
        for sign in (1, -1):
            to = moved(0, sign, 0) if r < 2 else moved(sign, 0, 0)
            pl.semaphore_signal(known.at[r], inc=1, device_id=(to, me), device_id_type=MESH)

    own_green = pltpu.make_async_copy(green, ext.at[:, pl.ds(HALO, rows), :], loc_sem.at[0])
    own_sigma = pltpu.make_async_copy(sigma, sig.at[pl.ds(2 * me, 2)], loc_sem.at[1])
    own_slab = pltpu.make_async_copy(slab, slab_v, loc_sem.at[2])
    own_nbt = pltpu.make_async_copy(nbt, nbt_v, loc_sem.at[3])
    own_slab.start()
    own_nbt.start()
    own_sigma.start()
    own_green.start()
    pl.semaphore_wait(barrier, 7)

    def at_up(dev, t):
        return 2 * lax.rem(dev - t + 2 * LEVELS, LEVELS)

    def at_down(dev, t):
        return 2 * lax.rem(dev + t, LEVELS) + 1

    def ring(side, t, c, src=None):
        dev = down if side else up
        m = (at_down if side else at_up)(dev, t)
        return pltpu.make_async_remote_copy(
            src_ref=sig.at[m, c] if src is None else src, dst_ref=sig.at[m, c],
            send_sem=sig_send.at[2 * side + c, t], recv_sem=sig_recv.at[2 * side + c, t],
            device_id=(en, dev), device_id_type=MESH,
        )

    def columns(m):
        return pl.ds(pl.multiple_of(m * BS, BS), BS)

    def halo(side, t, c):
        dev, src_row, dst_row = ((up, rows - HALO, 0), (down, 0, rows + HALO))[side]
        m = (at_down if c else at_up)(dev, t)
        return pltpu.make_async_remote_copy(
            src_ref=green.at[:, pl.ds(src_row, HALO), columns(m)],
            dst_ref=ext.at[:, pl.ds(dst_row, HALO), columns(m)],
            send_sem=halo_send.at[2 * side + c, t], recv_sem=halo_recv.at[2 * side + c, t],
            device_id=(en, dev), device_id_type=MESH,
        )

    for c in range(2):
        for side in range(2):
            ring(side, 1, c, sigma.at[side, c]).start()
    for t in range(2):
        for c in range(2):
            for side in range(2):
                halo(side, t, c).start()
    tell(0)

    own_slab.wait()
    own_nbt.wait()
    pairs = slab.shape[1]
    degree = nbt.shape[0]
    pick = (iota((pairs, BS), 0) == mine * degree + iota((pairs, BS), 1) // W).astype(F32)
    zed[...] = jnp.dot(slab_v[...], pick, preferred_element_type=F32, precision=HIGHEST)
    atoms = rows // W
    near = jnp.where(iota((degree, atoms), 1) == mine, nbt_v[...].astype(F32), 0.0)
    near = jnp.sum(near, axis=1, keepdims=True)
    off = jnp.where(
        iota((degree, BS), 0) == iota((degree, BS), 1) // W,
        jnp.broadcast_to(near, (degree, BS)), 0.0,
    )
    off = jnp.sum(off, axis=0, keepdims=True) - (me * atoms + mine).astype(F32)
    place = off + 8.0 - (off > 0.0).astype(F32)
    place = jnp.broadcast_to(place, (W, BS))
    lane_l = iota((W, BS), 1) % W
    for c in range(3):
        v = jnp.zeros((W, BS), F32)
        for i in range(W):
            v = jnp.where(lane_l == i, zed[pl.ds(c * 64 + i * W, W), :], v)
        for d in range(2 * W):
            bd[pl.ds(d * W, W), pl.ds(c * BS, BS)] = jnp.where(place == float(d), v, 0.0)
    delta = iota((ne, ne), 1) - iota((ne, ne), 0)
    k = jnp.zeros((ne, ne), F32)
    for q in range(shift.shape[0]):
        k = k + jnp.where(delta == shift[q], weight[0, q], 0.0)
        k = k + jnp.where(delta == -shift[q], weight[1, q], 0.0)
    kmat[...] = k
    acc[...] = jnp.zeros_like(acc)

    def widen(r, carry):
        tile = zed[pl.ds(pl.multiple_of(r * W, W), W), :]
        for j in range(W):
            zexp[r * W + j] = jnp.broadcast_to(tile[j:j + 1, :], (W, BS))
        return carry

    lax.fori_loop(0, 24, widen, 0)

    own_sigma.wait()
    own_green.wait()

    def block(m):
        cols = columns(m)
        x = jnp.concatenate([ext[0, :, cols], ext[1, :, cols]], axis=1)
        xh, xl = split(x)
        sr, si = sig[m, 0], sig[m, 1]
        w = jnp.concatenate(
            [jnp.concatenate([sr, si], axis=1), jnp.concatenate([-si, sr], axis=1)], axis=0
        )
        wh, wl = split(w)
        ph, pq = split(dot(xh, wh) + (dot(xh, wl) + dot(xl, wh)))

        def stacked(v):
            return jnp.concatenate(
                [v, jnp.concatenate([v[:, BS:], -v[:, :BS]], axis=1)], axis=0
            )

        for h in range(2):
            lo, c0 = h * half_rows, h * 2 * HALO
            lh = stacked(ph[lo:lo + half_rows])
            lq = stacked(pq[lo:lo + half_rows])
            bh, bq = xh[c0:c0 + 256], xl[c0:c0 + 256]
            acc[h] += dot_nt(lh, bh) + (dot_nt(lh, bq) + dot_nt(lq, bh))

    def due(t, c):
        for side in range(2):
            halo(side, t, c).wait_recv()
        block((at_down if c else at_up)(me, t))

    def step(t, carry):
        for c in range(2):
            for side in range(2):
                ring(side, t, c).wait_recv()
                ring(side, t + 1, c).start()
            for side in range(2):
                halo(side, t + 1, c).start()
            due(t - 1, c)
        for r in range(4):
            @pl.when(t == r + 1)
            def _():
                pl.semaphore_wait(known.at[r], 2)
                if r < 3:
                    tell(r + 1)
        return carry

    lax.fori_loop(1, LEVELS - 1, step, 0)

    def last(t, carry):
        @pl.when(t == LEVELS - 1)
        def _():
            for c in range(2):
                for side in range(2):
                    ring(side, t, c).wait_recv()

        due(t, 0)
        due(t, 1)
        return carry

    lax.fori_loop(LEVELS - 2, LEVELS, last, 0)

    lane = iota((W, BS), 1)

    def extract(h, i):
        s = ((64 if h == 0 else 224) - 8 * i) % 256
        s2 = (s - 8) % 256
        for z in range(2):
            x = acc[h, pl.ds(z * half_rows + 8 * i, W), :]
            y1 = pltpu.roll(x, s, 1)[:, :BS] if s else x[:, :BS]
            y2 = pltpu.roll(x, s2, 1)[:, :BS] if s2 else x[:, :BS]
            bx[h * 20 + i, pl.ds(z * W, W), :] = jnp.where(lane < 64, y1, y2)

    for i in range(4):
        extract(0, i)
        extract(1, 16 + i)
    own_rows = pl.ds(pl.multiple_of(en * 16, 16), 16)

    def beside(n):
        to, level = (atoms - 4 + n, down) if n < 4 else (n - 4, up)
        return pltpu.make_async_remote_copy(
            src_ref=pair.at[n], dst_ref=rcv_n.at[en],
            send_sem=n_send.at[n], recv_sem=n_recv.at[en],
            device_id=(device_of(to), level), device_id_type=MESH,
        )

    def from_beside(e):
        return pltpu.make_async_remote_copy(
            src_ref=pair.at[0], dst_ref=rcv_n.at[e],
            send_sem=n_send.at[0], recv_sem=n_recv.at[e],
            device_id=(en, up), device_id_type=MESH,
        )

    for n in range(4):
        re, im = bx[n, :W], pltpu.roll(bx[n, W:], 96, 1)
        pair[n] = jnp.where(lane >= 96, re, im)
        re, im = bx[atoms + 4 + n, :W], pltpu.roll(bx[atoms + 4 + n, W:], 32, 1)
        pair[4 + n] = jnp.where(lane < 32, re, im)
    for n in range(8):
        beside(n).start()
    for i in range(16):
        extract(0, 4 + i)
        extract(1, i)

    def there(d):
        return moved(*FAR_FIRST[d])

    def back(d):
        dy, dx, dc = FAR_FIRST[d]
        return moved(-dy, -dx, dc)

    def rows_of(e):
        return pl.ds(pl.multiple_of(e * 16, 16), 16)

    def spread(d, source=None):
        to = there(d)
        return pltpu.make_async_remote_copy(
            src_ref=bx.at[4 + atom_of(to)],
            dst_ref=rcv.at[own_rows if source is None else rows_of(source), :],
            send_sem=a_send.at[d], recv_sem=a_recv.at[d],
            device_id=(to, me), device_id_type=MESH,
        )

    for d in range(ne - 1):
        spread(d).start()
    rcv[own_rows, :] = bx[4 + mine]

    for d in range(ne - 1):
        spread(d, back(d)).wait_recv()

    @pl.when((mine < 4) | (mine >= atoms - 4))
    def _():
        def wait_beside(e, carry):
            from_beside(e).wait_recv()
            return carry

        lax.fori_loop(0, ne, wait_beside, 0)
        low = jnp.where(mine < 4, 8 * (4 - mine), 0)
        high = jnp.where(mine >= atoms - 4, 64 + 8 * (7 + atoms - 4 - mine), BS)
        take = (lane < low) | (lane >= high)
        for e in range(ne):
            re = rcv_n[e]
            im = jnp.where(mine < 4, pltpu.roll(re, 96, 1), pltpu.roll(re, 32, 1))
            for z, part in enumerate((re, im)):
                r = pl.ds(16 * e + W * z, W)
                rcv[r, :] = jnp.where(take, part, rcv[r, :])

    xs = jnp.concatenate([rcv[pl.ds(r, ne, stride=16), :] for r in range(16)], axis=1)
    xh, xq = split(xs)
    kh, kq = split(kmat[...])
    ys = dot(kh, xh) + (dot(kh, xq) + dot(kq, xh))
    yh, yq = split(jnp.concatenate([ys[:, r * BS:(r + 1) * BS] for r in range(16)], axis=0))
    bh, bq = split(bd[...])
    half[...] = dot(yh, bh) + (dot(yh, bq) + dot(yq, bh))

    def conjugate(tile):
        v = []
        for z in range(2):
            t = [
                half[
                    pl.ds((z * W + j) * ne + tile * W, W),
                    pl.ds(c * BS, BS),
                ]
                for c in range(3) for j in range(W)
            ]
            for i in range(W):
                total = [None, None]
                for c in range(3):
                    for j in range(W):
                        term = zexp[c * 64 + i * W + j] * t[c * W + j]
                        total[j % 2] = term if total[j % 2] is None else total[j % 2] + term
                v.append(total[0] + total[1])
        for b in (1, 2, 4, 8):
            keep_low = (lane // (W * b)) % 2 == 0
            new = list(v)
            for r in range(16):
                if not r & b:
                    new[r] = jnp.where(keep_low, v[r], pltpu.roll(v[r + b], W * b, 1))
                    new[r + b] = jnp.where(keep_low, pltpu.roll(v[r], BS - W * b, 1), v[r + b])
            v = new
        for k in range(16):
            done[pl.ds(tile * BS + k, W, stride=16), :] = v[k]

    for tile in range(ne // W):
        conjugate(tile)

    def back_home(d, source=None):
        to = there(d)
        return pltpu.make_async_remote_copy(
            src_ref=done.at[rows_of(to), :],
            dst_ref=out.at[rows_of(mine if source is None else atom_of(source)), :],
            send_sem=b_send.at[d], recv_sem=b_recv.at[d],
            device_id=(to, me), device_id_type=MESH,
        )

    for d in range(ne - 1):
        back_home(d).start()
    keep = pltpu.make_async_copy(done.at[own_rows, :], out.at[rows_of(mine), :], loc_sem.at[0])
    keep.start()

    for n in range(8):
        beside(n).wait_send()

    def drain_ring(t, carry):
        for c in range(2):
            for side in range(2):
                ring(side, t, c).wait_send()
        return carry

    lax.fori_loop(1, LEVELS, drain_ring, 0)

    def drain_halo(t, carry):
        for c in range(2):
            for side in range(2):
                halo(side, t, c).wait_send()
        return carry

    lax.fori_loop(0, LEVELS, drain_halo, 0)

    for d in range(ne - 1):
        spread(d).wait_send()
    for d in range(ne - 1):
        back_home(d, back(d)).wait_recv()
    for d in range(ne - 1):
        back_home(d).wait_send()
    keep.wait()


def per_device(green, sigma, neighbours, phonon_shift, phonon_weight, dham):
    ne = lax.axis_size("energy")
    rows, cols = green.shape[2], green.shape[3]
    atoms, degree = neighbours.shape
    pairs = atoms * degree
    half_rows = rows // 2 + HALO
    slab = dham.transpose(1, 2, 3, 0).reshape(192, pairs)
    anyspec = pl.BlockSpec(memory_space=pl.ANY)
    smem = pl.BlockSpec(memory_space=pltpu.SMEM)
    dma = pltpu.SemaphoreType.DMA
    banded = pl.pallas_call(
        functools.partial(main_kernel, ne),
        out_shape=jax.ShapeDtypeStruct((pairs, BS), F32),
        in_specs=[anyspec, anyspec, anyspec, anyspec, smem, smem],
        out_specs=anyspec,
        scratch_shapes=[
            pltpu.VMEM((2, rows + 2 * HALO, cols), F32),
            pltpu.VMEM((cols // BS, 2, BS, BS), F32),
            pltpu.VMEM((2, 2 * half_rows, 256), F32),
            pltpu.VMEM((atoms + 8, 2 * W, BS), F32),
            pltpu.VMEM((8, W, BS), F32),
            pltpu.VMEM((ne * 16, BS), F32),
            pltpu.VMEM((ne, W, BS), F32),
            pltpu.VMEM((ne * 16, 3 * BS), F32),
            pltpu.VMEM((ne * 16, BS), F32),
            pltpu.VMEM((192, pairs), F32),
            pltpu.VMEM((degree, atoms), jnp.int32),
            pltpu.VMEM((192, BS), F32),
            pltpu.VMEM((192, W, BS), F32),
            pltpu.VMEM((BS, 3 * BS), F32),
            pltpu.VMEM((ne, ne), F32),
            pltpu.SemaphoreType.REGULAR((4,)),
            dma((4,)),
            dma((4, LEVELS)), dma((4, LEVELS)),
            dma((4, LEVELS)), dma((4, LEVELS)),
            dma((8,)), dma((ne,)),
            dma((ne,)), dma((ne,)),
            dma((ne,)), dma((ne,)),
        ],
        compiler_params=pltpu.CompilerParams(
            collective_id=0, has_side_effects=True, vmem_limit_bytes=64_000_000
        ),
        name="lesser",
    )(green[0], sigma[0], slab, neighbours.T, phonon_shift, phonon_weight)
    return banded[None]


def solution(mesh):
    return jax.shard_map(
        per_device,
        mesh=mesh,
        in_specs=(
            P("energy", None, "orb", None),
            P("energy", "orb", None, None, None),
            P("orb", None),
            P(),
            P(),
            P("orb", None, None, None),
        ),
        out_specs=P("energy", "orb", None),
        check_vma=False,
    )
```

```python
import functools

import jax
import jax.numpy as jnp
from jax import lax
from jax.experimental import pallas as pl
from jax.experimental.pallas import tpu as pltpu
from jax.sharding import PartitionSpec as P

W = 8
BS = 128
HALO = 32
LEVELS = 8
SIDE = 4
MESH = pl.DeviceIdType.MESH
FAR_FIRST = sorted(
    ((dy, dx, dc) for dy in range(SIDE) for dx in range(SIDE) for dc in range(2) if dy or dx or dc),
    key=lambda o: -(min(o[0], SIDE - o[0]) + min(o[1], SIDE - o[1])),
)
HIGHEST = lax.Precision.HIGHEST
F32 = jnp.float32
BF16 = jnp.bfloat16


def device_of(a):
    return 2 * (a % 16) + a // 16


def split(x):
    high = x.astype(BF16)
    return high, (x - high.astype(F32)).astype(BF16)


def dot(a, b):
    return jnp.dot(a, b, preferred_element_type=F32)


def dot_nt(a, b):
    return lax.dot_general(a, b, (((1,), (1,)), ((), ())), preferred_element_type=F32)


def iota(shape, dim):
    return lax.broadcasted_iota(jnp.int32, shape, dim)


def main_kernel(
    ne, green, sigma, slab, nbt, shift, weight, out,
    ext, sig, acc, bx, pair, rcv, rcv_n, half, done, slab_v, nbt_v, zed, zexp, bd, bds, kmat, shift_s, weight_s, known,
    loc_sem, sig_send, sig_recv, halo_send, halo_recv, n_send, n_recv,
    a_send, a_recv, b_send, b_recv,
):
    en = lax.axis_index("energy")
    me = lax.axis_index("orb")
    up = lax.rem(me + 1, LEVELS)
    down = lax.rem(me + LEVELS - 1, LEVELS)
    rows = green.shape[1]
    half_rows = rows // 2 + HALO

    core, chip = lax.rem(en, 2), lax.div(en, 2)
    chip_x, chip_y = lax.rem(chip, SIDE), lax.div(chip, SIDE)
    at_y = [lax.rem(chip_y + n, SIDE) * SIDE for n in range(SIDE)]
    at_x = [lax.rem(chip_x + n, SIDE) for n in range(SIDE)]
    at_core = [core, 1 - core]

    def moved(dy, dx, dc):
        return (at_y[dy % SIDE] + at_x[dx % SIDE]) * 2 + at_core[dc % 2]

    def atom_moved(dy, dx, dc):
        return at_y[dy % SIDE] + at_x[dx % SIDE] + 16 * at_core[dc % 2]

    mine = atom_moved(0, 0, 0)

    barrier = pltpu.get_barrier_semaphore()
    for z in (up, down):
        pl.semaphore_signal(barrier, inc=1, device_id=(en, z), device_id_type=MESH)
    for step_to in ((0, 1, 0), (0, -1, 0), (1, 0, 0), (-1, 0, 0), (0, 0, 1)):
        pl.semaphore_signal(
            barrier, inc=1, device_id=(moved(*step_to), me), device_id_type=MESH
        )

    def tell(r):
        for sign in (1, -1):
            to = moved(0, sign, 0) if r < 2 else moved(sign, 0, 0)
            pl.semaphore_signal(known.at[r], inc=1, device_id=(to, me), device_id_type=MESH)

    own_green = pltpu.make_async_copy(green, ext.at[:, pl.ds(HALO, rows), :], loc_sem.at[0])
    own_sigma = pltpu.make_async_copy(sigma, sig.at[pl.ds(2 * me, 2)], loc_sem.at[1])
    own_slab = pltpu.make_async_copy(slab, slab_v, loc_sem.at[2])
    own_nbt = pltpu.make_async_copy(nbt, nbt_v, loc_sem.at[3])
    own_slab.start()
    own_nbt.start()
    own_shift = pltpu.make_async_copy(shift, shift_s, loc_sem.at[4])
    own_weight = pltpu.make_async_copy(weight, weight_s, loc_sem.at[5])
    own_shift.start()
    own_weight.start()
    own_sigma.start()
    own_green.start()
    pl.semaphore_wait(barrier, 7)

    def at_up(dev, t):
        return 2 * lax.rem(dev - t + 2 * LEVELS, LEVELS)

    def at_down(dev, t):
        return 2 * lax.rem(dev + t, LEVELS) + 1

    def ring(side, t, c, src=None):
        dev = down if side else up
        m = (at_down if side else at_up)(dev, t)
        return pltpu.make_async_remote_copy(
            src_ref=sig.at[m, c] if src is None else src, dst_ref=sig.at[m, c],
            send_sem=sig_send.at[2 * side + c, t], recv_sem=sig_recv.at[2 * side + c, t],
            device_id=(en, dev), device_id_type=MESH,
        )

    def columns(m):
        return pl.ds(pl.multiple_of(m * BS, BS), BS)

    def halo(side, t, c):
        dev, src_row, dst_row = ((up, rows - HALO, 0), (down, 0, rows + HALO))[side]
        m = (at_down if c else at_up)(dev, t)
        return pltpu.make_async_remote_copy(
            src_ref=green.at[:, pl.ds(src_row, HALO), columns(m)],
            dst_ref=ext.at[:, pl.ds(dst_row, HALO), columns(m)],
            send_sem=halo_send.at[2 * side + c, t], recv_sem=halo_recv.at[2 * side + c, t],
            device_id=(en, dev), device_id_type=MESH,
        )

    for c in range(2):
        for side in range(2):
            ring(side, 1, c, sigma.at[side, c]).start()
    for t in range(2):
        for c in range(2):
            for side in range(2):
                halo(side, t, c).start()
    tell(0)

    own_slab.wait()
    own_nbt.wait()
    own_shift.wait()
    own_weight.wait()
    pairs = slab.shape[1]
    degree = nbt.shape[0]
    pick = (iota((pairs, BS), 0) == mine * degree + iota((pairs, BS), 1) // W).astype(F32)
    zed[...] = jnp.dot(slab_v[...], pick, preferred_element_type=F32, precision=HIGHEST)
    atoms = rows // W
    near = jnp.where(iota((degree, atoms), 1) == mine, nbt_v[...].astype(F32), 0.0)
    near = jnp.sum(near, axis=1, keepdims=True)
    off = jnp.where(
        iota((degree, BS), 0) == iota((degree, BS), 1) // W,
        jnp.broadcast_to(near, (degree, BS)), 0.0,
    )
    off = jnp.sum(off, axis=0, keepdims=True) - (me * atoms + mine).astype(F32)
    place = off + 8.0 - (off > 0.0).astype(F32)
    place = jnp.broadcast_to(place, (W, BS))
    lane_l = iota((W, BS), 1) % W
    for c in range(3):
        v = jnp.zeros((W, BS), F32)
        for i in range(W):
            v = jnp.where(lane_l == i, zed[pl.ds(c * 64 + i * W, W), :], v)
        for d in range(2 * W):
            bd[pl.ds(d * W, W), pl.ds(c * BS, BS)] = jnp.where(place == float(d), v, 0.0)
    bds[0], bds[1] = split(bd[...])
    delta = iota((ne, ne), 1) - iota((ne, ne), 0)
    k = jnp.zeros((ne, ne), F32)
    for q in range(shift.shape[0]):
        k = k + jnp.where(delta == shift_s[q], weight_s[0, q], 0.0)
        k = k + jnp.where(delta == -shift_s[q], weight_s[1, q], 0.0)
    kmat[0], kmat[1] = split(k)
    acc[...] = jnp.zeros_like(acc)

    def widen(r, carry):
        tile = zed[pl.ds(pl.multiple_of(r * W, W), W), :]
        for j in range(W):
            zexp[r * W + j] = jnp.broadcast_to(tile[j:j + 1, :], (W, BS))
        return carry

    lax.fori_loop(0, 24, widen, 0)

    own_sigma.wait()
    own_green.wait()

    def block(m):
        cols = columns(m)
        x = jnp.concatenate([ext[0, :, cols], ext[1, :, cols]], axis=1)
        xh, xl = split(x)
        sr, si = sig[m, 0], sig[m, 1]
        w = jnp.concatenate(
            [jnp.concatenate([sr, si], axis=1), jnp.concatenate([-si, sr], axis=1)], axis=0
        )
        wh, wl = split(w)
        ph, pq = split(dot(xh, wh) + (dot(xh, wl) + dot(xl, wh)))

        def stacked(v):
            return jnp.concatenate(
                [v, jnp.concatenate([v[:, BS:], -v[:, :BS]], axis=1)], axis=0
            )

        for h in range(2):
            lo, c0 = h * half_rows, h * 2 * HALO
            lh = stacked(ph[lo:lo + half_rows])
            lq = stacked(pq[lo:lo + half_rows])
            bh, bq = xh[c0:c0 + 256], xl[c0:c0 + 256]
            acc[h] += dot_nt(lh, bh) + (dot_nt(lh, bq) + dot_nt(lq, bh))

    def due(t, c):
        for side in range(2):
            halo(side, t, c).wait_recv()
        block((at_down if c else at_up)(me, t))

    def step(t, carry):
        for c in range(2):
            for side in range(2):
                ring(side, t, c).wait_recv()
                ring(side, t + 1, c).start()
            for side in range(2):
                halo(side, t + 1, c).start()
            due(t - 1, c)
        for r in range(4):
            @pl.when(t == r + 1)
            def _():
                pl.semaphore_wait(known.at[r], 2)
                if r < 3:
                    tell(r + 1)
        return carry

    lax.fori_loop(1, LEVELS - 1, step, 0)

    def last(t, carry):
        @pl.when(t == LEVELS - 1)
        def _():
            for c in range(2):
                for side in range(2):
                    ring(side, t, c).wait_recv()

        due(t, 0)
        due(t, 1)
        return carry

    lax.fori_loop(LEVELS - 2, LEVELS, last, 0)

    lane = iota((W, BS), 1)

    def extract(h, i):
        s = ((64 if h == 0 else 224) - 8 * i) % 256
        s2 = (s - 8) % 256
        for z in range(2):
            x = acc[h, pl.ds(z * half_rows + 8 * i, W), :]
            y1 = pltpu.roll(x, s, 1)[:, :BS] if s else x[:, :BS]
            y2 = pltpu.roll(x, s2, 1)[:, :BS] if s2 else x[:, :BS]
            bx[h * 20 + i, pl.ds(z * W, W), :] = jnp.where(lane < 64, y1, y2)

    for i in range(4):
        extract(0, i)
        extract(1, 16 + i)
    own_rows = pl.ds(pl.multiple_of(en * 16, 16), 16)

    def beside(n):
        to, level = (atoms - 4 + n, down) if n < 4 else (n - 4, up)
        return pltpu.make_async_remote_copy(
            src_ref=pair.at[n], dst_ref=rcv_n.at[en],
            send_sem=n_send.at[n], recv_sem=n_recv.at[en],
            device_id=(device_of(to), level), device_id_type=MESH,
        )

    def from_beside(e):
        return pltpu.make_async_remote_copy(
            src_ref=pair.at[0], dst_ref=rcv_n.at[e],
            send_sem=n_send.at[0], recv_sem=n_recv.at[e],
            device_id=(en, up), device_id_type=MESH,
        )

    for n in range(4):
        re, im = bx[n, :W], pltpu.roll(bx[n, W:], 96, 1)
        pair[n] = jnp.where(lane >= 96, re, im)
        re, im = bx[atoms + 4 + n, :W], pltpu.roll(bx[atoms + 4 + n, W:], 32, 1)
        pair[4 + n] = jnp.where(lane < 32, re, im)
    for n in range(8):
        beside(n).start()
    for i in range(16):
        extract(0, 4 + i)
        extract(1, i)

    def there(d):
        return moved(*FAR_FIRST[d])

    def back(d):
        dy, dx, dc = FAR_FIRST[d]
        return -dy, -dx, dc

    def rows_of(e):
        return pl.ds(pl.multiple_of(e * 16, 16), 16)

    def spread(d, source=None):
        to = there(d)
        return pltpu.make_async_remote_copy(
            src_ref=bx.at[4 + atom_moved(*FAR_FIRST[d])],
            dst_ref=rcv.at[own_rows if source is None else rows_of(moved(*source)), :],
            send_sem=a_send.at[d], recv_sem=a_recv.at[d],
            device_id=(to, me), device_id_type=MESH,
        )

    for d in range(ne - 1):
        spread(d).start()
    rcv[own_rows, :] = bx[4 + mine]

    for d in range(ne - 1):
        spread(d, back(d)).wait_recv()

    @pl.when((mine < 4) | (mine >= atoms - 4))
    def _():
        def wait_beside(e, carry):
            from_beside(e).wait_recv()
            return carry

        lax.fori_loop(0, ne, wait_beside, 0)
        low = jnp.where(mine < 4, 8 * (4 - mine), 0)
        high = jnp.where(mine >= atoms - 4, 64 + 8 * (7 + atoms - 4 - mine), BS)
        take = (lane < low) | (lane >= high)
        for e in range(ne):
            re = rcv_n[e]
            im = jnp.where(mine < 4, pltpu.roll(re, 96, 1), pltpu.roll(re, 32, 1))
            for z, part in enumerate((re, im)):
                r = pl.ds(16 * e + W * z, W)
                rcv[r, :] = jnp.where(take, part, rcv[r, :])

    xs = jnp.concatenate([rcv[pl.ds(r, ne, stride=16), :] for r in range(16)], axis=1)
    xh, xq = split(xs)
    kh, kq = kmat[0], kmat[1]
    ys = dot(kh, xh) + (dot(kh, xq) + dot(kq, xh))
    yh, yq = split(jnp.concatenate([ys[:, r * BS:(r + 1) * BS] for r in range(16)], axis=0))
    bh, bq = bds[0], bds[1]
    half[...] = dot(yh, bh) + (dot(yh, bq) + dot(yq, bh))

    def conjugate(tile):
        v = []
        for z in range(2):
            t = [
                half[
                    pl.ds((z * W + j) * ne + tile * W, W),
                    pl.ds(c * BS, BS),
                ]
                for c in range(3) for j in range(W)
            ]
            for i in range(W):
                total = [None, None]
                for c in range(3):
                    for j in range(W):
                        term = zexp[c * 64 + i * W + j] * t[c * W + j]
                        total[j % 2] = term if total[j % 2] is None else total[j % 2] + term
                v.append(total[0] + total[1])
        for b in (1, 2, 4, 8):
            keep_low = (lane // (W * b)) % 2 == 0
            new = list(v)
            for r in range(16):
                if not r & b:
                    new[r] = jnp.where(keep_low, v[r], pltpu.roll(v[r + b], W * b, 1))
                    new[r + b] = jnp.where(keep_low, pltpu.roll(v[r], BS - W * b, 1), v[r + b])
            v = new
        for k in range(16):
            done[pl.ds(tile * BS + k, W, stride=16), :] = v[k]

    for tile in range(ne // W):
        conjugate(tile)

    def back_home(d, source=None):
        to = there(d)
        return pltpu.make_async_remote_copy(
            src_ref=done.at[rows_of(to), :],
            dst_ref=out.at[rows_of(mine if source is None else atom_moved(*source)), :],
            send_sem=b_send.at[d], recv_sem=b_recv.at[d],
            device_id=(to, me), device_id_type=MESH,
        )

    for d in range(ne - 1):
        back_home(d).start()
    keep = pltpu.make_async_copy(done.at[own_rows, :], out.at[rows_of(mine), :], loc_sem.at[0])
    keep.start()

    for n in range(8):
        beside(n).wait_send()

    def drain_ring(t, carry):
        for c in range(2):
            for side in range(2):
                ring(side, t, c).wait_send()
        return carry

    lax.fori_loop(1, LEVELS, drain_ring, 0)

    def drain_halo(t, carry):
        for c in range(2):
            for side in range(2):
                halo(side, t, c).wait_send()
        return carry

    lax.fori_loop(0, LEVELS, drain_halo, 0)

    for d in range(ne - 1):
        spread(d).wait_send()
    for d in range(ne - 1):
        back_home(d, back(d)).wait_recv()
    for d in range(ne - 1):
        back_home(d).wait_send()
    keep.wait()


def per_device(green, sigma, neighbours, phonon_shift, phonon_weight, dham):
    ne = lax.axis_size("energy")
    rows, cols = green.shape[2], green.shape[3]
    atoms, degree = neighbours.shape
    pairs = atoms * degree
    half_rows = rows // 2 + HALO
    slab = dham.transpose(1, 2, 3, 0).reshape(192, pairs)
    anyspec = pl.BlockSpec(memory_space=pl.ANY)
    dma = pltpu.SemaphoreType.DMA
    banded = pl.pallas_call(
        functools.partial(main_kernel, ne),
        out_shape=jax.ShapeDtypeStruct((pairs, BS), F32),
        in_specs=[anyspec] * 6,
        out_specs=anyspec,
        scratch_shapes=[
            pltpu.VMEM((2, rows + 2 * HALO, cols), F32),
            pltpu.VMEM((cols // BS, 2, BS, BS), F32),
            pltpu.VMEM((2, 2 * half_rows, 256), F32),
            pltpu.VMEM((atoms + 8, 2 * W, BS), F32),
            pltpu.VMEM((8, W, BS), F32),
            pltpu.VMEM((ne * 16, BS), F32),
            pltpu.VMEM((ne, W, BS), F32),
            pltpu.VMEM((ne * 16, 3 * BS), F32),
            pltpu.VMEM((ne * 16, BS), F32),
            pltpu.VMEM((192, pairs), F32),
            pltpu.VMEM((degree, atoms), jnp.int32),
            pltpu.VMEM((192, BS), F32),
            pltpu.VMEM((192, W, BS), F32),
            pltpu.VMEM((BS, 3 * BS), F32),
            pltpu.VMEM((2, BS, 3 * BS), BF16),
            pltpu.VMEM((2, ne, ne), BF16),
            pltpu.SMEM((6,), jnp.int32),
            pltpu.SMEM((2, 6), F32),
            pltpu.SemaphoreType.REGULAR((4,)),
            dma((6,)),
            dma((4, LEVELS)), dma((4, LEVELS)),
            dma((4, LEVELS)), dma((4, LEVELS)),
            dma((8,)), dma((ne,)),
            dma((ne,)), dma((ne,)),
            dma((ne,)), dma((ne,)),
        ],
        compiler_params=pltpu.CompilerParams(
            collective_id=0, has_side_effects=True, vmem_limit_bytes=40_000_000
        ),
        name="lesser",
    )(*(
        pltpu.with_memory_space_constraint(v, pltpu.HBM)
        for v in (green[0], sigma[0], slab, neighbours.T, phonon_shift, phonon_weight)
    ))
    return banded[None]


def solution(mesh):
    return jax.shard_map(
        per_device,
        mesh=mesh,
        in_specs=(
            P("energy", None, "orb", None),
            P("energy", "orb", None, None, None),
            P("orb", None),
            P(),
            P(),
            P("orb", None, None, None),
        ),
        out_specs=P("energy", "orb", None),
        check_vma=False,
    )
```

```python
import functools

import jax
import jax.numpy as jnp
from jax import lax
from jax.experimental import pallas as pl
from jax.experimental.pallas import tpu as pltpu
from jax.sharding import PartitionSpec as P

W = 8
BS = 128
HALO = 32
LEVELS = 8
SIDE = 4
MESH = pl.DeviceIdType.MESH
FAR_FIRST = sorted(
    ((dy, dx, dc) for dy in range(SIDE) for dx in range(SIDE) for dc in range(2) if dy or dx or dc),
    key=lambda o: -(min(o[0], SIDE - o[0]) + min(o[1], SIDE - o[1])),
)
HIGHEST = lax.Precision.HIGHEST
F32 = jnp.float32
BF16 = jnp.bfloat16


def device_of(a):
    return 2 * (a % 16) + a // 16


def split(x):
    high = x.astype(BF16)
    return high, (x - high.astype(F32)).astype(BF16)


def dot(a, b):
    return jnp.dot(a, b, preferred_element_type=F32)


def dot_nt(a, b):
    return lax.dot_general(a, b, (((1,), (1,)), ((), ())), preferred_element_type=F32)


def iota(shape, dim):
    return lax.broadcasted_iota(jnp.int32, shape, dim)


def main_kernel(
    ne, green, sigma, slab, nbt, shift, weight, out,
    ext, sig, acc, bx, pair, rcv, rcv_n, half, done, slab_v, nbt_v, zed, zexp, bd, bds, kmat, shift_s, weight_s, known,
    loc_sem, sig_send, sig_recv, halo_send, halo_recv, n_send, n_recv,
    a_send, a_recv, b_send, b_recv,
):
    en = lax.axis_index("energy")
    me = lax.axis_index("orb")
    up = lax.rem(me + 1, LEVELS)
    down = lax.rem(me + LEVELS - 1, LEVELS)
    rows = green.shape[1]
    half_rows = rows // 2 + HALO

    core, chip = lax.rem(en, 2), lax.div(en, 2)
    chip_x, chip_y = lax.rem(chip, SIDE), lax.div(chip, SIDE)
    at_y = [lax.rem(chip_y + n, SIDE) * SIDE for n in range(SIDE)]
    at_x = [lax.rem(chip_x + n, SIDE) for n in range(SIDE)]
    at_core = [core, 1 - core]

    def moved(dy, dx, dc):
        return (at_y[dy % SIDE] + at_x[dx % SIDE]) * 2 + at_core[dc % 2]

    def atom_moved(dy, dx, dc):
        return at_y[dy % SIDE] + at_x[dx % SIDE] + 16 * at_core[dc % 2]

    mine = atom_moved(0, 0, 0)

    barrier = pltpu.get_barrier_semaphore()
    for z in (up, down):
        pl.semaphore_signal(barrier, inc=1, device_id=(en, z), device_id_type=MESH)
    for step_to in ((0, 1, 0), (0, -1, 0), (1, 0, 0), (-1, 0, 0), (0, 0, 1)):
        pl.semaphore_signal(
            barrier, inc=1, device_id=(moved(*step_to), me), device_id_type=MESH
        )

    def tell(r):
        for sign in (1, -1):
            to = moved(0, sign, 0) if r < 2 else moved(sign, 0, 0)
            pl.semaphore_signal(known.at[r], inc=1, device_id=(to, me), device_id_type=MESH)

    own_green = pltpu.make_async_copy(green, ext.at[:, pl.ds(HALO, rows), :], loc_sem.at[0])
    own_sigma = pltpu.make_async_copy(sigma, sig.at[pl.ds(2 * me, 2)], loc_sem.at[1])
    own_slab = pltpu.make_async_copy(slab, slab_v, loc_sem.at[2])
    own_nbt = pltpu.make_async_copy(nbt, nbt_v, loc_sem.at[3])
    own_slab.start()
    own_nbt.start()
    own_shift = pltpu.make_async_copy(shift, shift_s, loc_sem.at[4])
    own_weight = pltpu.make_async_copy(weight, weight_s, loc_sem.at[5])
    own_shift.start()
    own_weight.start()
    own_sigma.start()
    own_green.start()
    pl.semaphore_wait(barrier, 7)

    def at_up(dev, t):
        return 2 * lax.rem(dev - t + 2 * LEVELS, LEVELS)

    def at_down(dev, t):
        return 2 * lax.rem(dev + t, LEVELS) + 1

    def ring(side, t, c, src=None):
        dev = down if side else up
        m = (at_down if side else at_up)(dev, t)
        return pltpu.make_async_remote_copy(
            src_ref=sig.at[m, c] if src is None else src, dst_ref=sig.at[m, c],
            send_sem=sig_send.at[2 * side + c, t], recv_sem=sig_recv.at[2 * side + c, t],
            device_id=(en, dev), device_id_type=MESH,
        )

    def columns(m):
        return pl.ds(pl.multiple_of(m * BS, BS), BS)

    def halo(side, t, c):
        dev, src_row, dst_row = ((up, rows - HALO, 0), (down, 0, rows + HALO))[side]
        m = (at_down if c else at_up)(dev, t)
        return pltpu.make_async_remote_copy(
            src_ref=green.at[:, pl.ds(src_row, HALO), columns(m)],
            dst_ref=ext.at[:, pl.ds(dst_row, HALO), columns(m)],
            send_sem=halo_send.at[2 * side + c, t], recv_sem=halo_recv.at[2 * side + c, t],
            device_id=(en, dev), device_id_type=MESH,
        )

    for c in range(2):
        for side in range(2):
            ring(side, 1, c, sigma.at[side, c]).start()
    for t in range(2):
        for c in range(2):
            for side in range(2):
                halo(side, t, c).start()
    tell(0)

    own_slab.wait()
    own_nbt.wait()
    own_shift.wait()
    own_weight.wait()
    pairs = slab.shape[1]
    degree = nbt.shape[0]
    pick = (iota((pairs, BS), 0) == mine * degree + iota((pairs, BS), 1) // W).astype(F32)
    zed[...] = jnp.dot(slab_v[...], pick, preferred_element_type=F32, precision=HIGHEST)
    atoms = rows // W
    near = jnp.where(iota((degree, atoms), 1) == mine, nbt_v[...].astype(F32), 0.0)
    near = jnp.sum(near, axis=1, keepdims=True)
    off = jnp.where(
        iota((degree, BS), 0) == iota((degree, BS), 1) // W,
        jnp.broadcast_to(near, (degree, BS)), 0.0,
    )
    off = jnp.sum(off, axis=0, keepdims=True) - (me * atoms + mine).astype(F32)
    place = off + 8.0 - (off > 0.0).astype(F32)
    place = jnp.broadcast_to(place, (W, BS))
    lane_l = iota((W, BS), 1) % W
    for c in range(3):
        v = jnp.zeros((W, BS), F32)
        for i in range(W):
            v = jnp.where(lane_l == i, zed[pl.ds(c * 64 + i * W, W), :], v)
        for d in range(2 * W):
            bd[pl.ds(d * W, W), pl.ds(c * BS, BS)] = jnp.where(place == float(d), v, 0.0)
    bds[0], bds[1] = split(bd[...])
    delta = iota((ne, ne), 1) - iota((ne, ne), 0)
    k = jnp.zeros((ne, ne), F32)
    for q in range(shift.shape[0]):
        k = k + jnp.where(delta == shift_s[q], weight_s[0, q], 0.0)
        k = k + jnp.where(delta == -shift_s[q], weight_s[1, q], 0.0)
    kmat[0], kmat[1] = split(k)
    acc[...] = jnp.zeros_like(acc)

    def widen(r, carry):
        tile = zed[pl.ds(pl.multiple_of(r * W, W), W), :]
        for j in range(W):
            zexp[r * W + j] = jnp.broadcast_to(tile[j:j + 1, :], (W, BS))
        return carry

    lax.fori_loop(0, 24, widen, 0)

    own_sigma.wait()
    own_green.wait()

    def block(m):
        cols = columns(m)
        x = jnp.concatenate([ext[0, :, cols], ext[1, :, cols]], axis=1)
        xh, xl = split(x)
        sr, si = sig[m, 0], sig[m, 1]
        w = jnp.concatenate(
            [jnp.concatenate([sr, si], axis=1), jnp.concatenate([-si, sr], axis=1)], axis=0
        )
        wh, wl = split(w)
        ph, pq = split(dot(xh, wh) + (dot(xh, wl) + dot(xl, wh)))

        def stacked(v):
            return jnp.concatenate(
                [v, jnp.concatenate([v[:, BS:], -v[:, :BS]], axis=1)], axis=0
            )

        for h in range(2):
            lo, c0 = h * half_rows, h * 2 * HALO
            lh = stacked(ph[lo:lo + half_rows])
            lq = stacked(pq[lo:lo + half_rows])
            bh, bq = xh[c0:c0 + 256], xl[c0:c0 + 256]
            acc[h] += dot_nt(lh, bh) + (dot_nt(lh, bq) + dot_nt(lq, bh))

    def due(t, c):
        for side in range(2):
            halo(side, t, c).wait_recv()
        block((at_down if c else at_up)(me, t))

    def step(t, carry):
        for c in range(2):
            for side in range(2):
                ring(side, t, c).wait_recv()
                ring(side, t + 1, c).start()
            for side in range(2):
                halo(side, t + 1, c).start()
            due(t - 1, c)
        for r in range(4):
            @pl.when(t == r + 1)
            def _():
                pl.semaphore_wait(known.at[r], 2)
                if r < 3:
                    tell(r + 1)
        return carry

    lax.fori_loop(1, LEVELS - 1, step, 0)

    def last(t, carry):
        @pl.when(t == LEVELS - 1)
        def _():
            for c in range(2):
                for side in range(2):
                    ring(side, t, c).wait_recv()

        due(t, 0)
        due(t, 1)
        return carry

    lax.fori_loop(LEVELS - 2, LEVELS, last, 0)

    lane = iota((W, BS), 1)

    def extract(h, i):
        s = ((64 if h == 0 else 224) - 8 * i) % 256
        s2 = (s - 8) % 256
        for z in range(2):
            x = acc[h, pl.ds(z * half_rows + 8 * i, W), :]
            y1 = pltpu.roll(x, s, 1)[:, :BS] if s else x[:, :BS]
            y2 = pltpu.roll(x, s2, 1)[:, :BS] if s2 else x[:, :BS]
            bx[h * 20 + i, pl.ds(z * W, W), :] = jnp.where(lane < 64, y1, y2)

    for i in range(4):
        extract(0, i)
        extract(1, 16 + i)
    own_rows = pl.ds(pl.multiple_of(en * 16, 16), 16)

    def beside(n):
        to, level = (atoms - 4 + n, down) if n < 4 else (n - 4, up)
        return pltpu.make_async_remote_copy(
            src_ref=pair.at[n], dst_ref=rcv_n.at[en],
            send_sem=n_send.at[n], recv_sem=n_recv.at[en],
            device_id=(device_of(to), level), device_id_type=MESH,
        )

    def from_beside(e):
        return pltpu.make_async_remote_copy(
            src_ref=pair.at[0], dst_ref=rcv_n.at[e],
            send_sem=n_send.at[0], recv_sem=n_recv.at[e],
            device_id=(en, up), device_id_type=MESH,
        )

    for n in range(4):
        re, im = bx[n, :W], pltpu.roll(bx[n, W:], 96, 1)
        pair[n] = jnp.where(lane >= 96, re, im)
        re, im = bx[atoms + 4 + n, :W], pltpu.roll(bx[atoms + 4 + n, W:], 32, 1)
        pair[4 + n] = jnp.where(lane < 32, re, im)
    for i in range(16):
        extract(0, 4 + i)
        extract(1, i)

    def there(d):
        return moved(*FAR_FIRST[d])

    def back(d):
        dy, dx, dc = FAR_FIRST[d]
        return -dy, -dx, dc

    def rows_of(e):
        return pl.ds(pl.multiple_of(e * 16, 16), 16)

    def spread(d, source=None):
        to = there(d)
        return pltpu.make_async_remote_copy(
            src_ref=bx.at[4 + atom_moved(*FAR_FIRST[d])],
            dst_ref=rcv.at[own_rows if source is None else rows_of(moved(*source)), :],
            send_sem=a_send.at[d], recv_sem=a_recv.at[d],
            device_id=(to, me), device_id_type=MESH,
        )

    for d in range(ne - 1):
        spread(d).start()
    for n in range(8):
        beside(n).start()
    rcv[own_rows, :] = bx[4 + mine]

    for d in range(ne - 1):
        spread(d, back(d)).wait_recv()

    @pl.when((mine < 4) | (mine >= atoms - 4))
    def _():
        def wait_beside(e, carry):
            from_beside(e).wait_recv()
            return carry

        lax.fori_loop(0, ne, wait_beside, 0)
        low = jnp.where(mine < 4, 8 * (4 - mine), 0)
        high = jnp.where(mine >= atoms - 4, 64 + 8 * (7 + atoms - 4 - mine), BS)
        take = (lane < low) | (lane >= high)
        for e in range(ne):
            re = rcv_n[e]
            im = jnp.where(mine < 4, pltpu.roll(re, 96, 1), pltpu.roll(re, 32, 1))
            for z, part in enumerate((re, im)):
                r = pl.ds(16 * e + W * z, W)
                rcv[r, :] = jnp.where(take, part, rcv[r, :])

    xs = jnp.concatenate([rcv[pl.ds(r, ne, stride=16), :] for r in range(16)], axis=1)
    xh, xq = split(xs)
    kh, kq = kmat[0], kmat[1]
    ys = dot(kh, xh) + (dot(kh, xq) + dot(kq, xh))
    yh, yq = split(jnp.concatenate([ys[:, r * BS:(r + 1) * BS] for r in range(16)], axis=0))
    bh, bq = bds[0], bds[1]
    half[...] = dot(yh, bh) + (dot(yh, bq) + dot(yq, bh))

    def conjugate(tile):
        v = []
        for z in range(2):
            t = [
                half[
                    pl.ds((z * W + j) * ne + tile * W, W),
                    pl.ds(c * BS, BS),
                ]
                for c in range(3) for j in range(W)
            ]
            for i in range(W):
                total = [None, None]
                for c in range(3):
                    for j in range(W):
                        term = zexp[c * 64 + i * W + j] * t[c * W + j]
                        total[j % 2] = term if total[j % 2] is None else total[j % 2] + term
                v.append(total[0] + total[1])
        for b in (1, 2, 4, 8):
            keep_low = (lane // (W * b)) % 2 == 0
            new = list(v)
            for r in range(16):
                if not r & b:
                    new[r] = jnp.where(keep_low, v[r], pltpu.roll(v[r + b], W * b, 1))
                    new[r + b] = jnp.where(keep_low, pltpu.roll(v[r], BS - W * b, 1), v[r + b])
            v = new
        for k in range(16):
            done[pl.ds(tile * BS + k, W, stride=16), :] = v[k]

    for tile in range(ne // W):
        conjugate(tile)

    def back_home(d, source=None):
        to = there(d)
        return pltpu.make_async_remote_copy(
            src_ref=done.at[rows_of(to), :],
            dst_ref=out.at[rows_of(mine if source is None else atom_moved(*source)), :],
            send_sem=b_send.at[d], recv_sem=b_recv.at[d],
            device_id=(to, me), device_id_type=MESH,
        )

    for d in range(ne - 1):
        back_home(d).start()
    keep = pltpu.make_async_copy(done.at[own_rows, :], out.at[rows_of(mine), :], loc_sem.at[0])
    keep.start()

    for n in range(8):
        beside(n).wait_send()

    def drain_ring(t, carry):
        for c in range(2):
            for side in range(2):
                ring(side, t, c).wait_send()
        return carry

    lax.fori_loop(1, LEVELS, drain_ring, 0)

    def drain_halo(t, carry):
        for c in range(2):
            for side in range(2):
                halo(side, t, c).wait_send()
        return carry

    lax.fori_loop(0, LEVELS, drain_halo, 0)

    for d in range(ne - 1):
        spread(d).wait_send()
    for d in range(ne - 1):
        back_home(d, back(d)).wait_recv()
    for d in range(ne - 1):
        back_home(d).wait_send()
    keep.wait()


def per_device(green, sigma, neighbours, phonon_shift, phonon_weight, dham):
    ne = lax.axis_size("energy")
    rows, cols = green.shape[2], green.shape[3]
    atoms, degree = neighbours.shape
    pairs = atoms * degree
    half_rows = rows // 2 + HALO
    slab = dham.transpose(1, 2, 3, 0).reshape(192, pairs)
    anyspec = pl.BlockSpec(memory_space=pl.ANY)
    dma = pltpu.SemaphoreType.DMA
    banded = pl.pallas_call(
        functools.partial(main_kernel, ne),
        out_shape=jax.ShapeDtypeStruct((pairs, BS), F32),
        in_specs=[anyspec] * 6,
        out_specs=anyspec,
        scratch_shapes=[
            pltpu.VMEM((2, rows + 2 * HALO, cols), F32),
            pltpu.VMEM((cols // BS, 2, BS, BS), F32),
            pltpu.VMEM((2, 2 * half_rows, 256), F32),
            pltpu.VMEM((atoms + 8, 2 * W, BS), F32),
            pltpu.VMEM((8, W, BS), F32),
            pltpu.VMEM((ne * 16, BS), F32),
            pltpu.VMEM((ne, W, BS), F32),
            pltpu.VMEM((ne * 16, 3 * BS), F32),
            pltpu.VMEM((ne * 16, BS), F32),
            pltpu.VMEM((192, pairs), F32),
            pltpu.VMEM((degree, atoms), jnp.int32),
            pltpu.VMEM((192, BS), F32),
            pltpu.VMEM((192, W, BS), F32),
            pltpu.VMEM((BS, 3 * BS), F32),
            pltpu.VMEM((2, BS, 3 * BS), BF16),
            pltpu.VMEM((2, ne, ne), BF16),
            pltpu.SMEM((6,), jnp.int32),
            pltpu.SMEM((2, 6), F32),
            pltpu.SemaphoreType.REGULAR((4,)),
            dma((6,)),
            dma((4, LEVELS)), dma((4, LEVELS)),
            dma((4, LEVELS)), dma((4, LEVELS)),
            dma((8,)), dma((ne,)),
            dma((ne,)), dma((ne,)),
            dma((ne,)), dma((ne,)),
        ],
        compiler_params=pltpu.CompilerParams(
            collective_id=0, has_side_effects=True, vmem_limit_bytes=40_000_000
        ),
        name="lesser",
    )(*(
        pltpu.with_memory_space_constraint(v, pltpu.HBM)
        for v in (green[0], sigma[0], slab, neighbours.T, phonon_shift, phonon_weight)
    ))
    return banded[None]


def solution(mesh):
    return jax.shard_map(
        per_device,
        mesh=mesh,
        in_specs=(
            P("energy", None, "orb", None),
            P("energy", "orb", None, None, None),
            P("orb", None),
            P(),
            P(),
            P("orb", None, None, None),
        ),
        out_specs=P("energy", "orb", None),
        check_vma=False,
    )
```

```python
import functools

import jax
import jax.numpy as jnp
from jax import lax
from jax.experimental import pallas as pl
from jax.experimental.pallas import tpu as pltpu
from jax.sharding import PartitionSpec as P

W = 8
BS = 128
HALO = 32
LEVELS = 8
SIDE = 4
MESH = pl.DeviceIdType.MESH
FAR_FIRST = sorted(
    ((dy, dx, dc) for dy in range(SIDE) for dx in range(SIDE) for dc in range(2) if dy or dx or dc),
    key=lambda o: -(min(o[0], SIDE - o[0]) + min(o[1], SIDE - o[1])),
)
HIGHEST = lax.Precision.HIGHEST
F32 = jnp.float32
BF16 = jnp.bfloat16


def device_of(a):
    return 2 * (a % 16) + a // 16


def split(x):
    high = x.astype(BF16)
    return high, (x - high.astype(F32)).astype(BF16)


def dot(a, b):
    return jnp.dot(a, b, preferred_element_type=F32)


def dot_nt(a, b):
    return lax.dot_general(a, b, (((1,), (1,)), ((), ())), preferred_element_type=F32)


def iota(shape, dim):
    return lax.broadcasted_iota(jnp.int32, shape, dim)


def main_kernel(
    ne, green, sigma, slab, nbt, shift, weight, out,
    ext, sig, acc, bx, pair, rcv, rcv_n, half, done, slab_v, nbt_v, zed, zexp, bd, bds, kmat, shift_s, weight_s, known,
    loc_sem, sig_send, sig_recv, halo_send, halo_recv, n_send, n_recv,
    a_send, a_recv, b_send, b_recv,
):
    en = lax.axis_index("energy")
    me = lax.axis_index("orb")
    up = lax.rem(me + 1, LEVELS)
    down = lax.rem(me + LEVELS - 1, LEVELS)
    rows = green.shape[1]
    half_rows = rows // 2 + HALO

    core, chip = lax.rem(en, 2), lax.div(en, 2)
    chip_x, chip_y = lax.rem(chip, SIDE), lax.div(chip, SIDE)
    at_y = [lax.rem(chip_y + n, SIDE) * SIDE for n in range(SIDE)]
    at_x = [lax.rem(chip_x + n, SIDE) for n in range(SIDE)]
    at_core = [core, 1 - core]

    def moved(dy, dx, dc):
        return (at_y[dy % SIDE] + at_x[dx % SIDE]) * 2 + at_core[dc % 2]

    def atom_moved(dy, dx, dc):
        return at_y[dy % SIDE] + at_x[dx % SIDE] + 16 * at_core[dc % 2]

    mine = atom_moved(0, 0, 0)

    barrier = pltpu.get_barrier_semaphore()
    for z in (up, down):
        pl.semaphore_signal(barrier, inc=1, device_id=(en, z), device_id_type=MESH)
    for step_to in ((0, 1, 0), (0, -1, 0), (1, 0, 0), (-1, 0, 0), (0, 0, 1)):
        pl.semaphore_signal(
            barrier, inc=1, device_id=(moved(*step_to), me), device_id_type=MESH
        )

    def tell(r):
        for sign in (1, -1):
            to = moved(0, sign, 0) if r < 2 else moved(sign, 0, 0)
            pl.semaphore_signal(known.at[r], inc=1, device_id=(to, me), device_id_type=MESH)

    own_green = pltpu.make_async_copy(green, ext.at[:, pl.ds(HALO, rows), :], loc_sem.at[0])
    own_sigma = pltpu.make_async_copy(sigma, sig.at[pl.ds(2 * me, 2)], loc_sem.at[1])
    own_slab = pltpu.make_async_copy(slab, slab_v, loc_sem.at[2])
    own_nbt = pltpu.make_async_copy(nbt, nbt_v, loc_sem.at[3])
    own_slab.start()
    own_nbt.start()
    own_shift = pltpu.make_async_copy(shift, shift_s, loc_sem.at[4])
    own_weight = pltpu.make_async_copy(weight, weight_s, loc_sem.at[5])
    own_shift.start()
    own_weight.start()
    own_sigma.start()
    own_green.start()
    pl.semaphore_wait(barrier, 7)

    def at_up(dev, t):
        return 2 * lax.rem(dev - t + 2 * LEVELS, LEVELS)

    def at_down(dev, t):
        return 2 * lax.rem(dev + t, LEVELS) + 1

    def ring(side, t, c, src=None):
        dev = down if side else up
        m = (at_down if side else at_up)(dev, t)
        return pltpu.make_async_remote_copy(
            src_ref=sig.at[m, c] if src is None else src, dst_ref=sig.at[m, c],
            send_sem=sig_send.at[2 * side + c, t], recv_sem=sig_recv.at[2 * side + c, t],
            device_id=(en, dev), device_id_type=MESH,
        )

    def columns(m):
        return pl.ds(pl.multiple_of(m * BS, BS), BS)

    def halo(side, t, c):
        dev, src_row, dst_row = ((up, rows - HALO, 0), (down, 0, rows + HALO))[side]
        m = (at_down if c else at_up)(dev, t)
        return pltpu.make_async_remote_copy(
            src_ref=green.at[:, pl.ds(src_row, HALO), columns(m)],
            dst_ref=ext.at[:, pl.ds(dst_row, HALO), columns(m)],
            send_sem=halo_send.at[2 * side + c, t], recv_sem=halo_recv.at[2 * side + c, t],
            device_id=(en, dev), device_id_type=MESH,
        )

    for c in range(2):
        for side in range(2):
            ring(side, 1, c, sigma.at[side, c]).start()
    for t in range(2):
        for c in range(2):
            for side in range(2):
                halo(side, t, c).start()
    tell(0)

    own_slab.wait()
    own_nbt.wait()
    own_shift.wait()
    own_weight.wait()
    pairs = slab.shape[1]
    degree = nbt.shape[0]
    pick = (iota((pairs, BS), 0) == mine * degree + iota((pairs, BS), 1) // W).astype(F32)
    zed[...] = jnp.dot(slab_v[...], pick, preferred_element_type=F32, precision=HIGHEST)
    atoms = rows // W
    near = jnp.where(iota((degree, atoms), 1) == mine, nbt_v[...].astype(F32), 0.0)
    near = jnp.sum(near, axis=1, keepdims=True)
    off = jnp.where(
        iota((degree, BS), 0) == iota((degree, BS), 1) // W,
        jnp.broadcast_to(near, (degree, BS)), 0.0,
    )
    off = jnp.sum(off, axis=0, keepdims=True) - (me * atoms + mine).astype(F32)
    place = off + 8.0 - (off > 0.0).astype(F32)
    place = jnp.broadcast_to(place, (W, BS))
    lane_l = iota((W, BS), 1) % W
    for c in range(3):
        v = jnp.zeros((W, BS), F32)
        for i in range(W):
            v = jnp.where(lane_l == i, zed[pl.ds(c * 64 + i * W, W), :], v)
        for d in range(2 * W):
            bd[pl.ds(d * W, W), pl.ds(c * BS, BS)] = jnp.where(place == float(d), v, 0.0)
    bds[0], bds[1] = split(bd[...])
    delta = iota((ne, ne), 1) - iota((ne, ne), 0)
    k = jnp.zeros((ne, ne), F32)
    for q in range(shift.shape[0]):
        k = k + jnp.where(delta == shift_s[q], weight_s[0, q], 0.0)
        k = k + jnp.where(delta == -shift_s[q], weight_s[1, q], 0.0)
    kmat[0], kmat[1] = split(k)
    acc[...] = jnp.zeros_like(acc)

    def widen(r, carry):
        tile = zed[pl.ds(pl.multiple_of(r * W, W), W), :]
        for j in range(W):
            zexp[r * W + j] = jnp.broadcast_to(tile[j:j + 1, :], (W, BS))
        return carry

    lax.fori_loop(0, 24, widen, 0)

    own_sigma.wait()
    own_green.wait()

    def block(m):
        cols = columns(m)
        x = jnp.concatenate([ext[0, :, cols], ext[1, :, cols]], axis=1)
        xh, xl = split(x)
        sr, si = sig[m, 0], sig[m, 1]
        w = jnp.concatenate(
            [jnp.concatenate([sr, si], axis=1), jnp.concatenate([-si, sr], axis=1)], axis=0
        )
        wh, wl = split(w)
        ph, pq = split(dot(xh, wh) + (dot(xh, wl) + dot(xl, wh)))

        def stacked(v):
            return jnp.concatenate(
                [v, jnp.concatenate([v[:, BS:], -v[:, :BS]], axis=1)], axis=0
            )

        for h in range(2):
            lo, c0 = h * half_rows, h * 2 * HALO
            lh = stacked(ph[lo:lo + half_rows])
            lq = stacked(pq[lo:lo + half_rows])
            bh, bq = xh[c0:c0 + 256], xl[c0:c0 + 256]
            acc[h] += dot_nt(lh, bh) + (dot_nt(lh, bq) + dot_nt(lq, bh))

    def due(t, c):
        for side in range(2):
            halo(side, t, c).wait_recv()
        block((at_down if c else at_up)(me, t))

    def step(t, carry):
        for c in range(2):
            for side in range(2):
                ring(side, t, c).wait_recv()
                ring(side, t + 1, c).start()
            for side in range(2):
                halo(side, t + 1, c).start()
            due(t - 1, c)
        for r in range(4):
            @pl.when(t == r + 1)
            def _():
                pl.semaphore_wait(known.at[r], 2)
                if r < 3:
                    tell(r + 1)
        return carry

    lax.fori_loop(1, LEVELS - 1, step, 0)

    def last(t, carry):
        @pl.when(t == LEVELS - 1)
        def _():
            for c in range(2):
                for side in range(2):
                    ring(side, t, c).wait_recv()

        due(t, 0)
        due(t, 1)
        return carry

    lax.fori_loop(LEVELS - 2, LEVELS, last, 0)

    lane = iota((W, BS), 1)

    def extract(h, i):
        s = ((64 if h == 0 else 224) - 8 * i) % 256
        s2 = (s - 8) % 256
        for z in range(2):
            x = acc[h, pl.ds(z * half_rows + 8 * i, W), :]
            y1 = pltpu.roll(x, s, 1)[:, :BS] if s else x[:, :BS]
            y2 = pltpu.roll(x, s2, 1)[:, :BS] if s2 else x[:, :BS]
            bx[h * 20 + i, pl.ds(z * W, W), :] = jnp.where(lane < 64, y1, y2)

    for i in range(4):
        extract(0, i)
        extract(1, 16 + i)
    own_rows = pl.ds(pl.multiple_of(en * 16, 16), 16)

    def beside(n):
        to, level = (atoms - 4 + n, down) if n < 4 else (n - 4, up)
        return pltpu.make_async_remote_copy(
            src_ref=pair.at[n], dst_ref=rcv_n.at[en],
            send_sem=n_send.at[n], recv_sem=n_recv.at[en],
            device_id=(device_of(to), level), device_id_type=MESH,
        )

    def from_beside(e):
        return pltpu.make_async_remote_copy(
            src_ref=pair.at[0], dst_ref=rcv_n.at[e],
            send_sem=n_send.at[0], recv_sem=n_recv.at[e],
            device_id=(en, up), device_id_type=MESH,
        )

    for n in range(4):
        re, im = bx[n, :W], pltpu.roll(bx[n, W:], 96, 1)
        pair[n] = jnp.where(lane >= 96, re, im)
        re, im = bx[atoms + 4 + n, :W], pltpu.roll(bx[atoms + 4 + n, W:], 32, 1)
        pair[4 + n] = jnp.where(lane < 32, re, im)
    for i in range(16):
        extract(0, 4 + i)
        extract(1, i)

    def there(d):
        return moved(*FAR_FIRST[d])

    def back(d):
        dy, dx, dc = FAR_FIRST[d]
        return -dy, -dx, dc

    def rows_of(e):
        return pl.ds(pl.multiple_of(e * 16, 16), 16)

    def spread(d, source=None):
        to = there(d)
        return pltpu.make_async_remote_copy(
            src_ref=bx.at[4 + atom_moved(*FAR_FIRST[d])],
            dst_ref=rcv.at[own_rows if source is None else rows_of(moved(*source)), :],
            send_sem=a_send.at[d], recv_sem=a_recv.at[d],
            device_id=(to, me), device_id_type=MESH,
        )

    for d in range(ne - 1):
        spread(d).start()
    for n in range(8):
        beside(n).start()
    rcv[own_rows, :] = bx[4 + mine]

    for d in range(ne - 1):
        spread(d, back(d)).wait_recv()

    @pl.when((mine < 4) | (mine >= atoms - 4))
    def _():
        def wait_beside(e, carry):
            from_beside(e).wait_recv()
            return carry

        lax.fori_loop(0, ne, wait_beside, 0)
        low = jnp.where(mine < 4, 8 * (4 - mine), 0)
        high = jnp.where(mine >= atoms - 4, 64 + 8 * (7 + atoms - 4 - mine), BS)
        take = (lane < low) | (lane >= high)
        for e in range(ne):
            re = rcv_n[e]
            im = jnp.where(mine < 4, pltpu.roll(re, 96, 1), pltpu.roll(re, 32, 1))
            for z, part in enumerate((re, im)):
                r = pl.ds(16 * e + W * z, W)
                rcv[r, :] = jnp.where(take, part, rcv[r, :])

    xs = jnp.concatenate([rcv[pl.ds(r, ne, stride=16), :] for r in range(16)], axis=1)
    xh, xq = split(xs)
    kh, kq = kmat[0], kmat[1]
    ys = dot(kh, xh) + (dot(kh, xq) + dot(kq, xh))
    yh, yq = split(jnp.concatenate([ys[:, r * BS:(r + 1) * BS] for r in range(16)], axis=0))
    bh, bq = bds[0], bds[1]
    half[...] = dot(yh, bh) + (dot(yh, bq) + dot(yq, bh))

    def conjugate(tile):
        v = []
        for z in range(2):
            t = [
                half[
                    pl.ds(pl.multiple_of((z * W + j) * ne + tile * W, W), W),
                    pl.ds(c * BS, BS),
                ]
                for c in range(3) for j in range(W)
            ]
            for i in range(W):
                total = [None, None]
                for c in range(3):
                    for j in range(W):
                        term = zexp[c * 64 + i * W + j] * t[c * W + j]
                        total[j % 2] = term if total[j % 2] is None else total[j % 2] + term
                v.append(total[0] + total[1])
        for b in (1, 2, 4, 8):
            keep_low = (lane // (W * b)) % 2 == 0
            new = list(v)
            for r in range(16):
                if not r & b:
                    new[r] = jnp.where(keep_low, v[r], pltpu.roll(v[r + b], W * b, 1))
                    new[r + b] = jnp.where(keep_low, pltpu.roll(v[r], BS - W * b, 1), v[r + b])
            v = new
        for k in range(16):
            done[pl.ds(tile * BS + k, W, stride=16), :] = v[k]

    for off in (2, 1):
        conjugate(lax.rem(chip_y + off, SIDE))

    def back_home(d, source=None):
        to = there(d)
        return pltpu.make_async_remote_copy(
            src_ref=done.at[rows_of(to), :],
            dst_ref=out.at[rows_of(mine if source is None else atom_moved(*source)), :],
            send_sem=b_send.at[d], recv_sem=b_recv.at[d],
            device_id=(to, me), device_id_type=MESH,
        )

    for d in range(ne - 1):
        if FAR_FIRST[d][0] in (1, 2):
            back_home(d).start()
    for off in (3, 0):
        conjugate(lax.rem(chip_y + off, SIDE))
    for d in range(ne - 1):
        if FAR_FIRST[d][0] not in (1, 2):
            back_home(d).start()
    keep = pltpu.make_async_copy(done.at[own_rows, :], out.at[rows_of(mine), :], loc_sem.at[0])
    keep.start()

    for n in range(8):
        beside(n).wait_send()

    def drain_ring(t, carry):
        for c in range(2):
            for side in range(2):
                ring(side, t, c).wait_send()
        return carry

    lax.fori_loop(1, LEVELS, drain_ring, 0)

    def drain_halo(t, carry):
        for c in range(2):
            for side in range(2):
                halo(side, t, c).wait_send()
        return carry

    lax.fori_loop(0, LEVELS, drain_halo, 0)

    for d in range(ne - 1):
        spread(d).wait_send()
    for d in range(ne - 1):
        back_home(d, back(d)).wait_recv()
    for d in range(ne - 1):
        back_home(d).wait_send()
    keep.wait()


def per_device(green, sigma, neighbours, phonon_shift, phonon_weight, dham):
    ne = lax.axis_size("energy")
    rows, cols = green.shape[2], green.shape[3]
    atoms, degree = neighbours.shape
    pairs = atoms * degree
    half_rows = rows // 2 + HALO
    slab = dham.transpose(1, 2, 3, 0).reshape(192, pairs)
    anyspec = pl.BlockSpec(memory_space=pl.ANY)
    dma = pltpu.SemaphoreType.DMA
    banded = pl.pallas_call(
        functools.partial(main_kernel, ne),
        out_shape=jax.ShapeDtypeStruct((pairs, BS), F32),
        in_specs=[anyspec] * 6,
        out_specs=anyspec,
        scratch_shapes=[
            pltpu.VMEM((2, rows + 2 * HALO, cols), F32),
            pltpu.VMEM((cols // BS, 2, BS, BS), F32),
            pltpu.VMEM((2, 2 * half_rows, 256), F32),
            pltpu.VMEM((atoms + 8, 2 * W, BS), F32),
            pltpu.VMEM((8, W, BS), F32),
            pltpu.VMEM((ne * 16, BS), F32),
            pltpu.VMEM((ne, W, BS), F32),
            pltpu.VMEM((ne * 16, 3 * BS), F32),
            pltpu.VMEM((ne * 16, BS), F32),
            pltpu.VMEM((192, pairs), F32),
            pltpu.VMEM((degree, atoms), jnp.int32),
            pltpu.VMEM((192, BS), F32),
            pltpu.VMEM((192, W, BS), F32),
            pltpu.VMEM((BS, 3 * BS), F32),
            pltpu.VMEM((2, BS, 3 * BS), BF16),
            pltpu.VMEM((2, ne, ne), BF16),
            pltpu.SMEM((6,), jnp.int32),
            pltpu.SMEM((2, 6), F32),
            pltpu.SemaphoreType.REGULAR((4,)),
            dma((6,)),
            dma((4, LEVELS)), dma((4, LEVELS)),
            dma((4, LEVELS)), dma((4, LEVELS)),
            dma((8,)), dma((ne,)),
            dma((ne,)), dma((ne,)),
            dma((ne,)), dma((ne,)),
        ],
        compiler_params=pltpu.CompilerParams(
            collective_id=0, has_side_effects=True, vmem_limit_bytes=40_000_000
        ),
        name="lesser",
    )(*(
        pltpu.with_memory_space_constraint(v, pltpu.HBM)
        for v in (green[0], sigma[0], slab, neighbours.T, phonon_shift, phonon_weight)
    ))
    return banded[None]


def solution(mesh):
    return jax.shard_map(
        per_device,
        mesh=mesh,
        in_specs=(
            P("energy", None, "orb", None),
            P("energy", "orb", None, None, None),
            P("orb", None),
            P(),
            P(),
            P("orb", None, None, None),
        ),
        out_specs=P("energy", "orb", None),
        check_vma=False,
    )
```
